512 devices in a mesh: attn: 8 (over y, core), exp: 16 (over z), seq: 4 (over x).
Axes of the slice: x: 4, y: 4, z: 16, core: 2. Of those that a mesh axis runs over, the one named last changes fastest.
Arguments:
- tokens: bfloat16 [256, 6144], P(('attn', 'exp'), 'seq'), may hold values from -6 to 6
- modality: int32 [256], P(('attn', 'exp')), may hold values from 0 to 1, as said below
- cotangent: bfloat16 [256, 6144], P(('attn', 'exp'), 'seq'), may hold values from -6 to 6
- gate_speech: bfloat16 [6144, 24576], P('seq', ('attn', 'exp')), may hold values from -0.078125 to 0.078125
- up_speech: bfloat16 [6144, 24576], P('seq', ('attn', 'exp')), may hold values from -0.078125 to 0.078125
- down_speech: bfloat16 [24576, 6144], P(('attn', 'exp'), 'seq'), may hold values from -0.078125 to 0.078125
- gate_text: bfloat16 [6144, 16384], P('seq', ('attn', 'exp')), may hold values from -0.078125 to 0.078125
- up_text: bfloat16 [6144, 16384], P('seq', ('attn', 'exp')), may hold values from -0.078125 to 0.078125
- down_text: bfloat16 [16384, 6144], P(('attn', 'exp'), 'seq'), may hold values from -0.09375 to 0.09375
Outputs:
- mixed: bfloat16 [256, 6144], P(('attn', 'exp'), 'seq')
- token_grad: bfloat16 [256, 6144], P(('attn', 'exp'), 'seq')
- down_speech_grad: bfloat16 [24576, 6144], P(('attn', 'exp'), 'seq')
- down_text_grad: bfloat16 [16384, 6144], P(('attn', 'exp'), 'seq')
The draws below stay inside these ranges and needn't reach their ends.
Inputs may be any that keep to these rules, and one draw needn't show every extreme that they name: Exactly 160 tokens of the window have modality 0 and the other 96 have modality 1, at places drawn from the seed.
All inputs are finite; a program needn't handle non-finite values.
Results may differ from the reference program's by a relative error of at most 0.005.
Values may be sent and summed in bfloat16 or wider, within the bound.
A program may use at most 64 MiB of HBM per device.

```python
import jax
import jax.numpy as jnp

D = 6144
FFS = 24576
FFT = 16384
TOKENS = 256
SPEECH = 160


def draw_modality(key, part):
    placed = jax.random.permutation(key, TOKENS)
    return (placed >= SPEECH).astype(jnp.int32)


def steps_of(stream_key, extent, split, low, high):
    def one(position, blocks):
        draws = jax.random.uniform(jax.random.fold_in(jax.random.fold_in(stream_key, 6), position), (blocks,), jnp.float32, low / len(split), high / len(split))
        return jnp.repeat(jnp.exp(draws), extent[position] // blocks).reshape((-1,) + (1,) * (len(extent) - position - 1))

    loudness = one(*split[0])
    for cut in split[1:]:
        loudness = loudness * one(*cut)
    return loudness


def noise(own_key, dims, width, bound, cuts=(), held_as=jnp.bfloat16):
    level = steps_of(own_key, dims, cuts, -0.22, 0.18) if cuts else 1.0
    entries = jax.random.normal(own_key, dims, jnp.float32) * width * level
    return jnp.minimum(jnp.maximum(entries, -bound), bound).astype(held_as)


def setup_inputs(seed: int = 0) -> dict:
    streams_of = jax.random.split(jax.random.key(seed), 10)
    tokens = noise(streams_of[0], (TOKENS, D), 1.0, 6.0, ((0, 128), (1, 4)))
    modality = draw_modality(jax.random.fold_in(streams_of[9], 71), 0)
    cotangent = noise(streams_of[2], (TOKENS, D), 1.0, 6.0, ((0, 128), (1, 4)))
    gate_speech = noise(streams_of[3], (D, FFS), D ** -0.5, 0.078125, ((0, 4), (1, 128)))
    up_speech = noise(streams_of[4], (D, FFS), D ** -0.5, 0.078125, ((0, 4), (1, 128)))
    down_speech = noise(streams_of[5], (FFS, D), (FFS // 4) ** -0.5, 0.078125, ((0, 128), (1, 4)))
    gate_text = noise(streams_of[6], (D, FFT), D ** -0.5, 0.078125, ((0, 4), (1, 128)))
    up_text = noise(streams_of[7], (D, FFT), D ** -0.5, 0.078125, ((0, 4), (1, 128)))
    down_text = noise(streams_of[8], (FFT, D), (FFT // 4) ** -0.5, 0.09375, ((0, 128), (1, 4)))
    return dict(tokens=tokens, modality=modality, cotangent=cotangent, gate_speech=gate_speech, up_speech=up_speech, down_speech=down_speech, gate_text=gate_text, up_text=up_text, down_text=down_text)


def reference(tokens, modality, cotangent, gate_speech, up_speech, down_speech, gate_text, up_text, down_text):
    speech = (modality == 0)[:, None]
    gs = jnp.dot(tokens, gate_speech, preferred_element_type=jnp.float32)
    us = jnp.dot(tokens, up_speech, preferred_element_type=jnp.float32)
    gt = jnp.dot(tokens, gate_text, preferred_element_type=jnp.float32)
    ut = jnp.dot(tokens, up_text, preferred_element_type=jnp.float32)
    hs = (jax.nn.silu(gs) * us).astype(jnp.bfloat16)
    ht = (jax.nn.silu(gt) * ut).astype(jnp.bfloat16)
    ys = jnp.dot(hs, down_speech, preferred_element_type=jnp.float32)
    yt = jnp.dot(ht, down_text, preferred_element_type=jnp.float32)
    mixed = jnp.where(speech, ys, yt).astype(jnp.bfloat16)
    zero = jnp.zeros_like(cotangent)
    cs = jnp.where(speech, cotangent, zero)
    ct = jnp.where(speech, zero, cotangent)
    dhs = jnp.dot(cs, down_speech.T, preferred_element_type=jnp.float32)
    dht = jnp.dot(ct, down_text.T, preferred_element_type=jnp.float32)
    sig_s = jax.nn.sigmoid(gs)
    sig_t = jax.nn.sigmoid(gt)
    dgs = (dhs * us * sig_s * (1.0 + gs * (1.0 - sig_s))).astype(jnp.bfloat16)
    dus = (dhs * jax.nn.silu(gs)).astype(jnp.bfloat16)
    dgt = (dht * ut * sig_t * (1.0 + gt * (1.0 - sig_t))).astype(jnp.bfloat16)
    dut = (dht * jax.nn.silu(gt)).astype(jnp.bfloat16)
    token_grad = jnp.dot(dgs, gate_speech.T, preferred_element_type=jnp.float32)
    token_grad = token_grad + jnp.dot(dus, up_speech.T, preferred_element_type=jnp.float32)
    token_grad = token_grad + jnp.dot(dgt, gate_text.T, preferred_element_type=jnp.float32)
    token_grad = token_grad + jnp.dot(dut, up_text.T, preferred_element_type=jnp.float32)
    down_speech_grad = jnp.dot(hs.T, cs, preferred_element_type=jnp.float32).astype(jnp.bfloat16)
    down_text_grad = jnp.dot(ht.T, ct, preferred_element_type=jnp.float32).astype(jnp.bfloat16)
    return mixed, token_grad.astype(jnp.bfloat16), down_speech_grad, down_text_grad
```

```python
import functools

import jax
import jax.numpy as jnp
from jax import lax
from jax.experimental import pallas as pl
from jax.experimental.pallas import tpu as pltpu
from jax.sharding import PartitionSpec as P

BF = jnp.bfloat16
F32 = jnp.float32
MESH = pl.DeviceIdType.MESH
LANE = 128
TOK, COT, OUT, GRAD = range(4)


def nn(left, right):
    return lax.dot_general(left, right, (((1,), (0,)), ((), ())), preferred_element_type=F32)


def nt(left, right):
    return lax.dot_general(left, right, (((1,), (1,)), ((), ())), preferred_element_type=F32)


def tn(left, right):
    return lax.dot_general(left, right, (((0,), (0,)), ((), ())), preferred_element_type=F32)


def remote(src, dst, send, recv, device):
    return pltpu.make_async_remote_copy(
        src_ref=src, dst_ref=dst, send_sem=send, recv_sem=recv, device_id=device, device_id_type=MESH
    )


def kernel(
    NY, E, S,
    tok, mod, cot, w_gs, w_us, w_ds, w_gt, w_ut, w_dt,
    mixed_o, grad_o, dsg_o, dtg_o,
    gs, us, gt, ut, down,
    tok_blk, cot_blk, tok_z, cot_z, flat, xt, ct,
    p1, p2, r1, r2, gu, hb, gb,
    sib_src, sib_dst, acc, y_src, y_dst, z_src, z_dst, hcat,
    wsem, zsem, ysem, csem, xsem,
):
    attn, z, x = lax.axis_index("attn"), lax.axis_index("exp"), lax.axis_index("seq")
    y, c = attn // 2, attn % 2
    other = 1 - c
    R, D = cot_blk.shape
    RB = E * R
    HALF = NY * RB
    CH = 2 * HALF // S
    FS, FT = gs.shape[0], gt.shape[1]
    FX = FS - FT
    NC = 256 if D % 256 == 0 else D

    local = [
        pltpu.make_async_copy(tok, tok_blk.at[:, pl.ds(0, D)], wsem.at[0]),
        pltpu.make_async_copy(cot, cot_blk, wsem.at[1]),
        pltpu.make_async_copy(w_gs, gs, wsem.at[2]),
        pltpu.make_async_copy(w_us, us, wsem.at[3]),
        pltpu.make_async_copy(w_gt, gt, wsem.at[4]),
        pltpu.make_async_copy(w_ut, ut, wsem.at[5]),
        pltpu.make_async_copy(w_ds.at[pl.ds(0, FT)], down.at[pl.ds(0, FT)], wsem.at[6]),
        pltpu.make_async_copy(w_dt, down.at[pl.ds(FT, FT)], wsem.at[7]),
        pltpu.make_async_copy(w_ds.at[pl.ds(FT, FX)], down.at[pl.ds(2 * FT, FX)], wsem.at[8]),
    ]
    for copy in local:
        copy.start()

    def greet(axis, count, me, scale, base):
        def body(d, _):
            peer = lax.rem(me + d, count)
            pl.semaphore_signal(
                barrier, inc=1, device_id={axis: peer * scale + base}, device_id_type=MESH
            )
            return 0

        lax.fori_loop(1, count, body, 0)

    barrier = pltpu.get_barrier_semaphore()
    greet("exp", E, z, 1, 0)
    greet("attn", NY, y, 2, c)
    greet("seq", S, x, 1, 0)
    pl.semaphore_signal(barrier, inc=1, device_id={"attn": y * 2 + other}, device_id_type=MESH)

    local[0].wait()
    kind = jnp.concatenate(
        [jnp.full((1, LANE), mod[i].astype(F32), F32) for i in range(R)], axis=0
    )
    tok_blk[:, D:] = kind.astype(BF)
    local[1].wait()
    pl.semaphore_wait(barrier, (E - 1) + (NY - 1) + (S - 1) + 1)

    def z_send(k, src, dst):
        def body(d, _):
            t = lax.rem(z + d, E)
            remote(src(t), dst.at[z], zsem.at[k, 0, t], zsem.at[k, 1, z], {"exp": t}).start()
            return 0

        lax.fori_loop(1, E, body, 0)

    def z_each(k, src, dst, recv):
        def body(d, _):
            t = lax.rem(z + d, E)
            copy = remote(src(t), dst.at[t], zsem.at[k, 0, t], zsem.at[k, 1, t], {"exp": t})
            copy.wait_recv() if recv else copy.wait_send()
            return 0

        lax.fori_loop(1, E, body, 0)

    def y_copy(k, t, src, dst, mark):
        return remote(src, dst, ysem.at[k, 0, t], ysem.at[k, 1, mark], {"attn": t * 2 + c})

    def c_copy(k, i, src, dst):
        return remote(src, dst, csem.at[k, 0, i], csem.at[k, 1, i], {"attn": y * 2 + other})

    def x_copy(k, t, src, dst, mark):
        return remote(src, dst, xsem.at[k, 0, t], xsem.at[k, 1, mark], {"seq": t})

    def ys():
        return [lax.rem(y + d, NY) for d in range(1, NY)]

    def xs():
        return [lax.rem(x + d, S) for d in range(1, S)]

    def block(ref, core, yy):
        return ref.at[pl.ds(pl.multiple_of(core * HALF + yy * RB, RB), RB)]

    def rows(ref, i):
        return ref.at[pl.ds(pl.multiple_of(i * CH, CH), CH)]

    z_send(TOK, lambda t: tok_blk, tok_z)
    z_send(COT, lambda t: cot_blk, cot_z)
    tok_z[z] = tok_blk[...]
    cot_z[z] = cot_blk[...]

    def assemble(k, blk, buf, whole):
        z_each(k, lambda t: blk, buf, True)
        width = blk.shape[1]
        for i in range(E):
            flat[i * R : (i + 1) * R, :width] = buf[i].astype(F32)
        mine = block(whole, c, y)
        mine[...] = flat[:, :width].astype(BF)
        for t in ys():
            y_copy(k, t, mine, mine, y).start()
        c_copy(k, y, mine, mine).start()

    assemble(TOK, tok_blk, tok_z, xt)
    assemble(COT, cot_blk, cot_z, ct)

    def pass_on(k, whole):
        for t in ys():
            got = block(whole, c, t)
            y_copy(k, t, got, got, t).wait_recv()
            c_copy(k, t, got, got).start()

    def from_sibling(k, whole):
        for t in range(NY):
            got = block(whole, other, t)
            c_copy(k, t, got, got).wait_recv()

    def half_rows(core):
        return pl.ds(pl.multiple_of(core * HALF, HALF), HALF)

    def project(core):
        r = half_rows(core)
        feats = xt[r, :D]
        speech = xt[r, D:].astype(F32) < 0.5
        a, b = nt(feats, gs[...]), nt(feats, us[...])
        p1[r, 0:FT] = jnp.where(speech, a[:, :FT], nn(feats, gt[...]))
        p1[r, FT : 2 * FT] = jnp.where(speech, b[:, :FT], nn(feats, ut[...]))
        p1[r, 2 * FT :] = jnp.concatenate([a[:, FT:], b[:, FT:]], axis=1)

    def hidden_grad(core):
        r = half_rows(core)
        speech = xt[r, D:].astype(F32) < 0.5
        d = nt(ct[r, :], down[...])
        p2[r, 0:FT] = jnp.where(speech, d[:, :FT], d[:, FT : 2 * FT])
        tail = d[:, 2 * FT :]
        p2[r, FT:] = jnp.concatenate([tail, jnp.zeros_like(tail)], axis=1)

    for copy in local[2:6]:
        copy.wait()
    pass_on(TOK, xt)
    project(c)
    from_sibling(TOK, xt)
    project(other)
    for t in xs():
        x_copy(0, t, rows(p1, t), r1.at[x], x).start()

    for copy in local[6:]:
        copy.wait()
    pass_on(COT, ct)
    hidden_grad(c)
    from_sibling(COT, ct)
    hidden_grad(other)
    for t in xs():
        x_copy(1, t, rows(p2, t), r2.at[x], x).start()

    def split(v):
        return v[:, :FX], v[:, FX : 2 * FX]

    total = rows(p1, x)[...]
    for t in xs():
        x_copy(0, t, r1.at[t], r1.at[t], t).wait_recv()
        total += r1[t]
    gu[...] = total
    g, u = total[:, :FT], total[:, FT : 2 * FT]
    ge, ue = split(total[:, 2 * FT :])
    he = jax.nn.silu(ge) * ue
    mine = rows(hb, x)
    mine[:, 0:FT] = (jax.nn.silu(g) * u).astype(BF)
    mine[:, FT:] = jnp.concatenate([he, jnp.zeros_like(he)], axis=1).astype(BF)
    for t in xs():
        x_copy(2, t, mine, mine, x).start()

    total = rows(p2, x)[...]
    for t in xs():
        x_copy(1, t, r2.at[t], r2.at[t], t).wait_recv()
        total += r2[t]

    def back(dh, g, u):
        sig = jax.nn.sigmoid(g)
        return dh * u * sig * (1.0 + g * (1.0 - sig)), dh * (g * sig)

    dg, du = back(total[:, :FT], gu[:, :FT], gu[:, FT : 2 * FT])
    ge, ue = split(gu[:, 2 * FT :])
    dge, due = back(total[:, FT : FT + FX], ge, ue)
    mine_g = rows(gb, x)
    mine_g[:, 0:FT] = dg.astype(BF)
    mine_g[:, FT : 2 * FT] = du.astype(BF)
    mine_g[:, 2 * FT :] = jnp.concatenate([dge, due], axis=1).astype(BF)
    for t in xs():
        x_copy(3, t, mine_g, mine_g, x).start()

    def columns(n):
        return pl.ds(pl.multiple_of(n * NC, NC), NC)

    def out_half(core, store):
        r = half_rows(core)
        text = xt[r, D:]
        speech = (1.0 - text.astype(F32)).astype(BF)
        h = hb[r, 0:FT]
        hcat[r, 0:FT] = h * speech
        hcat[r, FT : 2 * FT] = h * text
        hcat[r, 2 * FT :] = hb[r, FT : FT + FX] * speech[:, :FX]
        left = hcat[r, :]

        def body(n, _):
            store(n, nn(left, down[:, columns(n)]))
            return 0

        lax.fori_loop(0, D // NC, body, 0)

    def grad_half(core, store):
        r = half_rows(core)
        text = xt[r, D:]
        speech = (1.0 - text.astype(F32)).astype(BF)
        dg, du = gb[r, 0:FT], gb[r, FT : 2 * FT]
        dge, due = split(gb[r, 2 * FT :])
        dgs = jnp.concatenate([dg * speech, dge * speech[:, :FX]], axis=1)
        dus = jnp.concatenate([du * speech, due * speech[:, :FX]], axis=1)
        dgt, dut = dg * text, du * text

        def body(n, _):
            w = columns(n)
            store(
                n,
                nn(dgs, gs[:, w]) + nn(dus, us[:, w]) + nt(dgt, gt[w, :]) + nt(dut, ut[w, :]),
            )
            return 0

        lax.fori_loop(0, D // NC, body, 0)

    def partials(k, half):
        def to_sibling(n, v):
            sib_src[k, :, columns(n)] = v.astype(BF)

        def keep(n, v):
            acc[k, :, columns(n)] = v

        half(other, to_sibling)
        c_copy(2 + k, 0, sib_src.at[k], sib_dst.at[k]).start()
        half(c, keep)

    def over_y(k):
        c_copy(2 + k, 0, sib_src.at[k], sib_dst.at[k]).wait_recv()

        def body(n, _):
            w = columns(n)
            v = acc[k, :, w] + sib_dst[k, :, w].astype(F32)
            acc[k, :, w] = v
            y_src[k, :, w] = v.astype(BF)
            return 0

        lax.fori_loop(0, D // NC, body, 0)
        for t in ys():
            y_copy(2 + k, t, y_part(y_src, k, t), y_dst.at[k, y], y).start()

    def y_part(ref, k, t):
        return ref.at[k, pl.ds(pl.multiple_of(t * RB, RB), RB)]

    def over_z(k):
        total = y_part(acc, k, y)[...]
        for t in ys():
            y_copy(2 + k, t, y_dst.at[k, t], y_dst.at[k, t], t).wait_recv()
            total += y_dst[k, t].astype(F32)
        for i in range(E):
            z_src[k, i] = total[i * R : (i + 1) * R].astype(BF)
        z_send(2 + k, lambda t: z_src.at[k, t], z_dst.at[k])
        z_dst[k, z] = z_src[k, z]

    def finish(k, out):
        z_each(2 + k, lambda t: z_src.at[k, t], z_dst.at[k], True)
        total = z_dst[k, 0].astype(F32)
        for i in range(1, E):
            total += z_dst[k, i].astype(F32)
        out[...] = total.astype(BF)

    for t in xs():
        got = rows(hb, t)
        x_copy(2, t, got, got, t).wait_recv()
    partials(0, out_half)
    for t in xs():
        got = rows(gb, t)
        x_copy(3, t, got, got, t).wait_recv()
    over_y(0)
    partials(1, grad_half)
    over_y(1)

    def down_grad(n, _):
        w = columns(n)
        v = tn(hcat[...], ct[:, w]).astype(BF)
        dsg_o[0:FT, w] = v[0:FT]
        dtg_o[:, w] = v[FT : 2 * FT]
        dsg_o[FT:, w] = v[2 * FT :]
        return 0

    lax.fori_loop(0, D // NC, down_grad, 0)

    over_z(0)
    over_z(1)
    finish(0, mixed_o)
    finish(1, grad_o)

    z_each(TOK, lambda t: tok_blk, tok_z, False)
    z_each(COT, lambda t: cot_blk, cot_z, False)
    for k in range(2):
        z_each(2 + k, lambda t: z_src.at[k, t], z_dst.at[k], False)
    mine = block(xt, c, y)
    mine_c = block(ct, c, y)
    for t in ys():
        y_copy(TOK, t, mine, mine, t).wait_send()
        y_copy(COT, t, mine_c, mine_c, t).wait_send()
        for k in range(2):
            y_copy(2 + k, t, y_part(y_src, k, t), y_dst.at[k, t], t).wait_send()
    for t in range(NY):
        got, got_c = block(xt, c, t), block(ct, c, t)
        c_copy(TOK, t, got, got).wait_send()
        c_copy(COT, t, got_c, got_c).wait_send()
    for k in range(2):
        c_copy(2 + k, 0, sib_src.at[k], sib_dst.at[k]).wait_send()
    for t in xs():
        x_copy(0, t, rows(p1, t), r1.at[t], t).wait_send()
        x_copy(1, t, rows(p2, t), r2.at[t], t).wait_send()
        got, got_g = rows(hb, x), rows(gb, x)
        x_copy(2, t, got, got, t).wait_send()
        x_copy(3, t, got_g, got_g, t).wait_send()


def shards(NY, E, S, tokens, modality, cotangent, *weights):
    R, D = tokens.shape
    gs, us, ds, gt, ut, dt = weights
    gs, us = gs.T, us.T
    FS, FT = gs.shape[0], gt.shape[1]
    RB = E * R
    HALF = NY * RB
    T = 2 * HALF
    CH = T // S
    DMA = pltpu.SemaphoreType.DMA
    hbm_spec = pl.BlockSpec(memory_space=pltpu.HBM)
    vmem_spec = pl.BlockSpec(memory_space=pltpu.VMEM)
    return pl.pallas_call(
        functools.partial(kernel, NY, E, S),
        out_shape=(
            jax.ShapeDtypeStruct((R, D), BF),
            jax.ShapeDtypeStruct((R, D), BF),
            jax.ShapeDtypeStruct(ds.shape, BF),
            jax.ShapeDtypeStruct(dt.shape, BF),
        ),
        in_specs=[hbm_spec, pl.BlockSpec(memory_space=pltpu.SMEM)] + [hbm_spec] * 7,
        out_specs=[vmem_spec] * 4,
        scratch_shapes=[
            pltpu.VMEM(gs.shape, BF),
            pltpu.VMEM(us.shape, BF),
            pltpu.VMEM(gt.shape, BF),
            pltpu.VMEM(ut.shape, BF),
            pltpu.VMEM((FS + FT, D), BF),
            pltpu.VMEM((R, D + LANE), BF),
            pltpu.VMEM((R, D), BF),
            pltpu.VMEM((E, R, D + LANE), BF),
            pltpu.VMEM((E, R, D), BF),
            pltpu.VMEM((RB, D + LANE), F32),
            pltpu.VMEM((T, D + LANE), BF),
            pltpu.VMEM((T, D), BF),
            pltpu.VMEM((T, 3 * FT), F32),
            pltpu.VMEM((T, 2 * FT), F32),
            pltpu.VMEM((S, CH, 3 * FT), F32),
            pltpu.VMEM((S, CH, 2 * FT), F32),
            pltpu.VMEM((CH, 3 * FT), F32),
            pltpu.VMEM((T, 2 * FT), BF),
            pltpu.VMEM((T, 3 * FT), BF),
            pltpu.VMEM((2, HALF, D), BF),
            pltpu.VMEM((2, HALF, D), BF),
            pltpu.VMEM((2, HALF, D), F32),
            pltpu.VMEM((2, HALF, D), BF),
            pltpu.VMEM((2, NY, RB, D), BF),
            pltpu.VMEM((2, E, R, D), BF),
            pltpu.VMEM((2, E, R, D), BF),
            pltpu.VMEM((T, FS + FT), BF),
            DMA((9,)),
            DMA((4, 2, E)),
            DMA((4, 2, NY)),
            DMA((4, 2, NY)),
            DMA((4, 2, S)),
        ],
        compiler_params=pltpu.CompilerParams(
            collective_id=0, has_side_effects=True, vmem_limit_bytes=62 << 20
        ),
    )(tokens, modality, cotangent, gs, us, ds, gt, ut, dt)


def solution(mesh):
    NY, E, S = mesh.shape["attn"] // 2, mesh.shape["exp"], mesh.shape["seq"]
    row = P(("attn", "exp"), "seq")
    col = P("seq", ("attn", "exp"))
    return jax.shard_map(
        functools.partial(shards, NY, E, S),
        mesh=mesh,
        in_specs=(row, P(("attn", "exp")), row, col, col, row, col, col, row),
        out_specs=(row, row, row, row),
        check_vma=False,
    )
```

```python
import functools

import jax
import jax.numpy as jnp
from jax import lax
from jax.experimental import pallas as pl
from jax.experimental.pallas import tpu as pltpu
from jax.sharding import PartitionSpec as P

BF = jnp.bfloat16
F32 = jnp.float32
MESH = pl.DeviceIdType.MESH
LANE = 128
TOK, COT = range(2)


def nn(left, right):
    return lax.dot_general(left, right, (((1,), (0,)), ((), ())), preferred_element_type=F32)


def nt(left, right):
    return lax.dot_general(left, right, (((1,), (1,)), ((), ())), preferred_element_type=F32)


def far_first(count):
    return sorted(range(1, count), key=lambda d: -min(d, count - d))


def remote(src, dst, send, recv, device):
    return pltpu.make_async_remote_copy(
        src_ref=src, dst_ref=dst, send_sem=send, recv_sem=recv, device_id=device, device_id_type=MESH
    )


def kernel(
    NY, E, S,
    tok, mod, cot, w_gs, w_us, w_ds, w_gt, w_ut, w_dt,
    mixed_o, grad_o, dsg_o, dtg_o,
    gt, ut, wide, down,
    tok_blk, cot_blk, tok_z, cot_z, flat, xt, ct,
    p1, p2, p2b, r1, r2, gu, hb, gb,
    sib_src, sib_dst, acc, y_src, y_dst, z_src, z_dst, hcat, mixed, grad, dsg, dtg,
    wsem, osem, zsem, ysem, gsem, csem, xsem,
):
    attn, z, x = lax.axis_index("attn"), lax.axis_index("exp"), lax.axis_index("seq")
    y, c = attn // 2, attn % 2
    other = 1 - c
    R, D = cot_blk.shape
    RB = E * R
    RG = RB // 2
    HALF = NY * RB
    CH = 2 * HALF // S
    FS, FT = w_gs.shape[0], gt.shape[1]
    FX = FS - FT
    NC = 512 if D % 512 == 0 else D

    def load(src, at, size, dst, to, n):
        return pltpu.make_async_copy(src.at[pl.ds(at, size)], dst.at[pl.ds(to, size)], wsem.at[n])

    local = [
        pltpu.make_async_copy(tok, tok_blk.at[:, pl.ds(0, D)], wsem.at[0]),
        pltpu.make_async_copy(cot, cot_blk, wsem.at[1]),
        pltpu.make_async_copy(w_gt, gt, wsem.at[2]),
        pltpu.make_async_copy(w_ut, ut, wsem.at[3]),
        load(w_gs, 0, FT, wide, 0, 4),
        load(w_us, 0, FT, wide, FT, 5),
        load(w_gs, FT, FX, wide, 4 * FT, 6),
        load(w_us, FT, FX, wide, 4 * FT + FX, 7),
        load(w_ds, 0, FT, down, 0, 8),
        load(w_dt, 0, FT, down, FT, 9),
        load(w_ds, FT, FX, down, 2 * FT, 10),
    ]
    for copy in local:
        copy.start()
    stores = [
        pltpu.make_async_copy(dsg, dsg_o, osem.at[0]),
        pltpu.make_async_copy(dtg, dtg_o, osem.at[1]),
        pltpu.make_async_copy(mixed, mixed_o, osem.at[2]),
        pltpu.make_async_copy(grad, grad_o, osem.at[3]),
    ]

    def greet(axis, count, me, scale, base):
        def body(d, _):
            peer = lax.rem(me + d, count)
            pl.semaphore_signal(
                barrier, inc=1, device_id={axis: peer * scale + base}, device_id_type=MESH
            )
            return 0

        lax.fori_loop(1, count, body, 0)

    barrier = pltpu.get_barrier_semaphore()
    greet("exp", E, z, 1, 0)
    greet("attn", NY, y, 2, c)
    greet("seq", S, x, 1, 0)
    pl.semaphore_signal(barrier, inc=1, device_id={"attn": y * 2 + other}, device_id_type=MESH)

    local[0].wait()
    kind = jnp.concatenate(
        [jnp.full((1, LANE), mod[i].astype(F32), F32) for i in range(R)], axis=0
    )
    tok_blk[:, D:] = kind.astype(BF)
    local[1].wait()
    pl.semaphore_wait(barrier, (E - 1) + (NY - 1) + (S - 1) + 1)

    def ahead(s):
        return lax.rem(z + E + (s + 1) // 2 * (2 * (s % 2) - 1), E)

    def mirror(s):
        return jnp.where(s == E - 1, s, s + 2 * (s % 2) - 1)

    pending = []

    def drain():
        for wait in pending:
            wait()

    def go(copy):
        copy.start()
        pending.append(copy.wait_send)

    def z_copy(k, s, src, dst, to):
        return remote(src(s), dst.at[to], zsem.at[k, 0, s], zsem.at[k, 1, to], {"exp": ahead(s)})

    def z_send(k, src, dst, low, high):
        def start(i, _):
            s = high - 1 - i
            z_copy(k, s, src, dst, mirror(s)).start()
            return 0

        def wait(s, _):
            z_copy(k, s, src, dst, s).wait_send()
            return 0

        lax.fori_loop(0, high - low, start, 0)
        pending.append(lambda: lax.fori_loop(low, high, wait, 0))

    def z_wait(k, src, dst, low, high):
        def wait(s, _):
            z_copy(k, s, src, dst, s).wait_recv()
            return 0

        lax.fori_loop(low, high, wait, 0)

    def y_copy(k, group, t, src, dst, mark):
        return remote(
            src, dst, ysem.at[k, group, 0, t], ysem.at[k, group, 1, mark], {"attn": t * 2 + c}
        )

    def g_copy(k, group, i, ref):
        return remote(
            ref, ref, gsem.at[k, group, 0, i], gsem.at[k, group, 1, i], {"attn": y * 2 + other}
        )

    def c_copy(k, n):
        w = pl.ds(n * NC, NC)
        return remote(
            sib_src.at[k, :, w], sib_dst.at[k, :, w], csem.at[k, 0, n], csem.at[k, 1, n],
            {"attn": y * 2 + other},
        )

    def x_copy(k, t, src, dst, mark):
        return remote(src, dst, xsem.at[k, 0, t], xsem.at[k, 1, mark], {"seq": t})

    def ys():
        return [lax.rem(y + d, NY) for d in far_first(NY)]

    def xs():
        return [lax.rem(x + d, S) for d in far_first(S)]

    def block(ref, core, yy, group):
        return ref.at[pl.ds(pl.multiple_of(core * HALF + yy * RB + group * RG, RG), RG)]

    def rows(ref, i):
        return ref.at[pl.ds(pl.multiple_of(i * CH, CH), CH)]

    z_send(TOK, lambda s: tok_blk, tok_z, 1, E)
    z_send(COT, lambda s: cot_blk, cot_z, 1, E)
    tok_z[0] = tok_blk[...]
    cot_z[0] = cot_blk[...]
    local[2].wait()
    wide[2 * FT : 3 * FT, :] = gt[...].T
    local[3].wait()
    wide[3 * FT : 4 * FT, :] = ut[...].T

    def assemble(k, group, blk, buf, whole):
        low = group * (E // 2)
        z_wait(k, lambda s: blk, buf, max(low, 1), low + E // 2)
        width = blk.shape[1]
        for i in range(E // 2):
            flat[i * R : (i + 1) * R, :width] = buf[low + i].astype(F32)
        mine = block(whole, c, y, group)
        mine[...] = flat[:, :width].astype(BF)
        for t in ys():
            go(y_copy(k, group, t, mine, mine, y))
        go(g_copy(k, group, y, mine))

    def pass_on(k, group, whole):
        for t in reversed(ys()):
            got = block(whole, c, t, group)
            y_copy(k, group, t, got, got, t).wait_recv()
            go(g_copy(k, group, t, got))

    def from_sibling(k, whole):
        for group in range(2):
            for t in range(NY):
                g_copy(k, group, t, block(whole, other, t, group)).wait_recv()

    def half_rows(core):
        return pl.ds(pl.multiple_of(core * HALF, HALF), HALF)

    def project(core):
        r = half_rows(core)
        v = nt(xt[r, :D], wide[...])
        speech = xt[r, D:].astype(F32) < 0.5
        p1[r, 0:FT] = jnp.where(speech, v[:, :FT], v[:, 2 * FT : 3 * FT])
        p1[r, FT : 2 * FT] = jnp.where(speech, v[:, FT : 2 * FT], v[:, 3 * FT : 4 * FT])
        p1[r, 2 * FT :] = v[:, 4 * FT :]

    def hidden_grad(core):
        r = half_rows(core)
        speech = xt[r, D:].astype(F32) < 0.5
        v = nt(ct[r, :], down[...])
        near = jnp.where(speech, v[:, :FT], v[:, FT : 2 * FT])
        tail = v[:, 2 * FT :]
        tail = jnp.concatenate([tail, jnp.zeros_like(tail)], axis=1)
        p2[r, 0:FT] = near
        p2[r, FT:] = tail
        p2b[r, 0:FT] = near.astype(BF)
        p2b[r, FT:] = tail.astype(BF)

    assemble(TOK, 0, tok_blk, tok_z, xt)
    assemble(TOK, 1, tok_blk, tok_z, xt)
    assemble(COT, 0, cot_blk, cot_z, ct)
    for copy in local[4:]:
        copy.wait()
    pass_on(TOK, 0, xt)
    assemble(COT, 1, cot_blk, cot_z, ct)
    pass_on(TOK, 1, xt)
    project(c)
    from_sibling(TOK, xt)
    project(other)
    for t in xs():
        go(x_copy(0, t, rows(p1, t), r1.at[x], x))
    pass_on(COT, 0, ct)
    pass_on(COT, 1, ct)
    hidden_grad(c)
    from_sibling(COT, ct)
    hidden_grad(other)
    for t in xs():
        go(x_copy(1, t, rows(p2b, t), r2.at[x], x))

    def split(v):
        return v[:, :FX], v[:, FX : 2 * FX]

    total = rows(p1, x)[...]
    for t in xs():
        x_copy(0, t, r1.at[t], r1.at[t], t).wait_recv()
        total += r1[t]
    gu[...] = total
    g, u = total[:, :FT], total[:, FT : 2 * FT]
    ge, ue = split(total[:, 2 * FT :])
    he = jax.nn.silu(ge) * ue
    mine = rows(hb, x)
    mine[:, 0:FT] = (jax.nn.silu(g) * u).astype(BF)
    mine[:, FT:] = jnp.concatenate([he, jnp.zeros_like(he)], axis=1).astype(BF)
    for t in xs():
        go(x_copy(2, t, mine, mine, x))

    total = rows(p2, x)[...]
    for t in xs():
        x_copy(1, t, r2.at[t], r2.at[t], t).wait_recv()
        total += r2[t].astype(F32)

    def back(dh, g, u):
        sig = jax.nn.sigmoid(g)
        return dh * u * sig * (1.0 + g * (1.0 - sig)), dh * (g * sig)

    dg, du = back(total[:, :FT], gu[:, :FT], gu[:, FT : 2 * FT])
    ge, ue = split(gu[:, 2 * FT :])
    dge, due = back(total[:, FT : FT + FX], ge, ue)
    mine_g = rows(gb, x)
    mine_g[:, 0:FT] = dg.astype(BF)
    mine_g[:, FT : 2 * FT] = du.astype(BF)
    mine_g[:, 2 * FT :] = jnp.concatenate([dge, due], axis=1).astype(BF)
    for t in xs():
        go(x_copy(3, t, mine_g, mine_g, x))

    def kinds(r):
        text = xt[r, D:]
        return (1.0 - text.astype(F32)).astype(BF), text

    def out_left(core):
        r = half_rows(core)
        speech, text = kinds(r)
        h = hb[r, 0:FT]
        hcat[r, 0:FT] = h * speech
        hcat[r, FT : 2 * FT] = h * text
        hcat[r, 2 * FT :] = hb[r, FT : FT + FX] * speech[:, :FX]
        return hcat[r, :]

    def grad_left(core):
        r = half_rows(core)
        speech, text = kinds(r)
        dg, du = gb[r, 0:FT], gb[r, FT : 2 * FT]
        return jnp.concatenate(
            [dg * speech, du * speech, dg * text, du * text, gb[r, 2 * FT :] * speech], axis=1
        )

    def partials(k, left, weights):
        rows_other = left(other)
        for n in range(D // NC):
            w = slice(n * NC, (n + 1) * NC)
            sib_src[k, :, w] = nn(rows_other, weights[:, w]).astype(BF)
            go(c_copy(k, n))
        rows_own = left(c)
        for n in range(D // NC):
            w = slice(n * NC, (n + 1) * NC)
            acc[k, :, w] = nn(rows_own, weights[:, w])

    def part(ref, k, t, group):
        return ref.at[k, pl.ds(pl.multiple_of(t * RB + group * RG, RG), RG)]

    def over_y(k):
        for n in range(D // NC):
            c_copy(k, n).wait_recv()
        for group in (1, 0):
            for t in ys():
                v = part(acc, k, t, group)[...] + part(sib_dst, k, t, group)[...].astype(F32)
                part(y_src, k, t, group)[...] = v.astype(BF)
                go(y_copy(2 + k, group, t, part(y_src, k, t, group), y_dst.at[k, group, y], y))

    def over_z(k):
        for group in (1, 0):
            total = part(acc, k, y, group)[...] + part(sib_dst, k, y, group)[...].astype(F32)
            for t in reversed(ys()):
                got = y_dst.at[k, group, t]
                y_copy(2 + k, group, t, got, got, t).wait_recv()
                total += got[...].astype(F32)
            low = group * (E // 2)
            for i in range(E // 2):
                z_src[k, low + i] = total[i * R : (i + 1) * R].astype(BF)
            z_send(2 + k, lambda s: z_src.at[k, s], z_dst.at[k], max(low, 1), low + E // 2)

    def finish(k, out):
        z_wait(2 + k, lambda s: z_src.at[k, s], z_dst.at[k], 1, E)
        total = z_src[k, 0].astype(F32)
        for i in range(1, E):
            total += z_dst[k, i].astype(F32)
        out[...] = total.astype(BF)

    def down_grads():
        left = hcat[...].T

        def body(n, _):
            w = pl.ds(pl.multiple_of(n * NC, NC), NC)
            v = nn(left, ct[:, w]).astype(BF)
            dsg[0:FT, w] = v[0:FT]
            dtg[:, w] = v[FT : 2 * FT]
            dsg[FT:, w] = v[2 * FT :]
            return 0

        lax.fori_loop(0, D // NC, body, 0)
        stores[0].start()
        stores[1].start()

    for t in xs():
        got = rows(hb, t)
        x_copy(2, t, got, got, t).wait_recv()
    partials(0, out_left, down)
    over_y(0)
    down_grads()
    for t in xs():
        got = rows(gb, t)
        x_copy(3, t, got, got, t).wait_recv()
    partials(1, grad_left, wide)
    over_y(1)
    over_z(0)
    over_z(1)
    finish(0, mixed)
    stores[2].start()
    finish(1, grad)
    stores[3].start()

    drain()
    for copy in stores:
        copy.wait()


def place(*refs):
    hold, sem = refs[8:12], refs[12]
    loads, stores = [], []
    for src, dst, mid in zip(refs[:4], refs[4:8], hold):
        strip = 64 if src.shape[0] % 64 == 0 else src.shape[0]
        for i in range(0, src.shape[0], strip):
            part, n = pl.ds(i, strip), len(loads)
            loads.append(pltpu.make_async_copy(src.at[part], mid.at[part], sem.at[0, n]))
            stores.append(pltpu.make_async_copy(mid.at[part], dst.at[part], sem.at[1, n]))
    for load in loads:
        load.start()
    for load, store in zip(loads, stores):
        load.wait()
        store.start()
    for store in stores:
        store.wait()


def shards(NY, E, S, tokens, modality, cotangent, *weights):
    R, D = tokens.shape
    gs, us, ds, gt, ut, dt = weights
    gs, us = gs.T, us.T
    FS, FT = gs.shape[0], gt.shape[1]
    RB = E * R
    HALF = NY * RB
    T = 2 * HALF
    CH = T // S
    DMA = pltpu.SemaphoreType.DMA
    hbm_spec = pl.BlockSpec(memory_space=pltpu.HBM)
    out_shape = (
        jax.ShapeDtypeStruct((R, D), BF),
        jax.ShapeDtypeStruct((R, D), BF),
        jax.ShapeDtypeStruct(ds.shape, BF),
        jax.ShapeDtypeStruct(dt.shape, BF),
    )
    outs = pl.pallas_call(
        functools.partial(kernel, NY, E, S),
        out_shape=out_shape,
        in_specs=[hbm_spec, pl.BlockSpec(memory_space=pltpu.SMEM)] + [hbm_spec] * 7,
        out_specs=[hbm_spec] * 4,
        scratch_shapes=[
            pltpu.VMEM(gt.shape, BF),
            pltpu.VMEM(ut.shape, BF),
            pltpu.VMEM((2 * (FS + FT), D), BF),
            pltpu.VMEM((FS + FT, D), BF),
            pltpu.VMEM((R, D + LANE), BF),
            pltpu.VMEM((R, D), BF),
            pltpu.VMEM((E, R, D + LANE), BF),
            pltpu.VMEM((E, R, D), BF),
            pltpu.VMEM((RB // 2, D + LANE), F32),
            pltpu.VMEM((T, D + LANE), BF),
            pltpu.VMEM((T, D), BF),
            pltpu.VMEM((T, 3 * FT), F32),
            pltpu.VMEM((T, 2 * FT), F32),
            pltpu.VMEM((T, 2 * FT), BF),
            pltpu.VMEM((S, CH, 3 * FT), F32),
            pltpu.VMEM((S, CH, 2 * FT), BF),
            pltpu.VMEM((CH, 3 * FT), F32),
            pltpu.VMEM((T, 2 * FT), BF),
            pltpu.VMEM((T, 3 * FT), BF),
            pltpu.VMEM((2, HALF, D), BF),
            pltpu.VMEM((2, HALF, D), BF),
            pltpu.VMEM((2, HALF, D), F32),
            pltpu.VMEM((2, HALF, D), BF),
            pltpu.VMEM((2, 2, NY, RB // 2, D), BF),
            pltpu.VMEM((2, E, R, D), BF),
            pltpu.VMEM((2, E, R, D), BF),
            pltpu.VMEM((T, FS + FT), BF),
            pltpu.VMEM((R, D), BF),
            pltpu.VMEM((R, D), BF),
            pltpu.VMEM(ds.shape, BF),
            pltpu.VMEM(dt.shape, BF),
            DMA((11,)),
            DMA((4,)),
            DMA((4, 2, E)),
            DMA((4, 2, 2, NY)),
            DMA((2, 2, 2, NY)),
            DMA((2, 2, 8)),
            DMA((4, 2, S)),
        ],
        compiler_params=pltpu.CompilerParams(
            collective_id=0, has_side_effects=True, vmem_limit_bytes=62 << 20
        ),
    )(tokens, modality, cotangent, gs, us, ds, gt, ut, dt)
    return pl.pallas_call(
        place,
        out_shape=out_shape,
        in_specs=[hbm_spec] * 4,
        out_specs=[hbm_spec] * 4,
        scratch_shapes=[pltpu.VMEM(o.shape, BF) for o in out_shape] + [DMA((2, 16))],
        compiler_params=pltpu.CompilerParams(vmem_limit_bytes=62 << 20),
    )(*outs)


def solution(mesh):
    NY, E, S = mesh.shape["attn"] // 2, mesh.shape["exp"], mesh.shape["seq"]
    row = P(("attn", "exp"), "seq")
    col = P("seq", ("attn", "exp"))
    return jax.shard_map(
        functools.partial(shards, NY, E, S),
        mesh=mesh,
        in_specs=(row, P(("attn", "exp")), row, col, col, row, col, col, row),
        out_specs=(row, row, row, row),
        check_vma=False,
    )
```

```python
import functools

import jax
import jax.numpy as jnp
from jax import lax
from jax.experimental import pallas as pl
from jax.experimental.pallas import tpu as pltpu
from jax.sharding import PartitionSpec as P

BF = jnp.bfloat16
F32 = jnp.float32
MESH = pl.DeviceIdType.MESH
LANE = 128
TOK, COT = range(2)


def nn(left, right):
    return lax.dot_general(left, right, (((1,), (0,)), ((), ())), preferred_element_type=F32)


def nt(left, right):
    return lax.dot_general(left, right, (((1,), (1,)), ((), ())), preferred_element_type=F32)


def far_first(count):
    return sorted(range(1, count), key=lambda d: -min(d, count - d))


def remote(src, dst, send, recv, device):
    return pltpu.make_async_remote_copy(
        src_ref=src, dst_ref=dst, send_sem=send, recv_sem=recv, device_id=device, device_id_type=MESH
    )


def kernel(
    NY, E, S,
    tok, mod, cot, w_gs, w_us, w_ds, w_gt, w_ut, w_dt,
    z_dst, dsg_o, dtg_o,
    gt, ut, wide, down,
    tok_blk, cot_blk, tok_z, cot_z, flat, xt, ct,
    p1, p2, p2b, r1, r2, gu, hb, gb,
    sib_src, sib_dst, acc, y_src, y_dst, z_src, hcat, dsg, dtg,
    wsem, osem, zsem, ysem, gsem, csem, xsem,
):
    attn, z, x = lax.axis_index("attn"), lax.axis_index("exp"), lax.axis_index("seq")
    y, c = attn // 2, attn % 2
    other = 1 - c
    R, D = cot_blk.shape
    RB = E * R
    RG = RB // 2
    HALF = NY * RB
    CH = 2 * HALF // S
    FS, FT = w_gs.shape[0], gt.shape[1]
    FX = FS - FT
    NC = 512 if D % 512 == 0 else D
    W = E // 4

    barrier = pltpu.get_barrier_semaphore()

    def greet(device):
        pl.semaphore_signal(barrier, inc=1, device_id=device, device_id_type=MESH)

    for k in range(W, 0, -1):
        greet({"exp": lax.rem(z + k, E)})
        greet({"exp": lax.rem(z + E - k, E)})
    for d in far_first(NY):
        greet({"attn": lax.rem(y + d, NY) * 2 + c})
    for d in far_first(S):
        greet({"seq": lax.rem(x + d, S)})
    greet({"attn": y * 2 + other})

    def load(src, at, size, dst, to, n):
        return pltpu.make_async_copy(src.at[pl.ds(at, size)], dst.at[pl.ds(to, size)], wsem.at[n])

    local = [
        pltpu.make_async_copy(tok, tok_blk.at[:, pl.ds(0, D)], wsem.at[0]),
        pltpu.make_async_copy(cot, cot_blk, wsem.at[1]),
        pltpu.make_async_copy(w_gt, gt, wsem.at[2]),
        pltpu.make_async_copy(w_ut, ut, wsem.at[3]),
        load(w_gs, 0, FT, wide, 0, 4),
        load(w_us, 0, FT, wide, FT, 5),
        load(w_gs, FT, FX, wide, 4 * FT, 6),
        load(w_us, FT, FX, wide, 4 * FT + FX, 7),
        load(w_ds, 0, FT, down, 0, 8),
        load(w_dt, 0, FT, down, FT, 9),
        load(w_ds, FT, FX, down, 2 * FT, 10),
    ]
    for copy in local:
        copy.start()
    stores = [
        pltpu.make_async_copy(dsg, dsg_o, osem.at[0]),
        pltpu.make_async_copy(dtg, dtg_o, osem.at[1]),
        pltpu.make_async_copy(z_src.at[0, 0], z_dst.at[0, 0], osem.at[2]),
        pltpu.make_async_copy(z_src.at[1, 0], z_dst.at[1, 0], osem.at[3]),
    ]

    local[0].wait()
    kind = jnp.concatenate(
        [jnp.full((1, LANE), mod[i].astype(F32), F32) for i in range(R)], axis=0
    )
    tok_blk[:, D:] = kind.astype(BF)
    local[1].wait()
    pl.semaphore_wait(barrier, 2 * W + (NY - 1) + (S - 1) + 1)

    def ahead(s):
        return lax.rem(z + E + (s + 1) // 2 * (2 * (s % 2) - 1), E)

    def mirror(s):
        return jnp.where(s == E - 1, s, s + 2 * (s % 2) - 1)

    pending = []

    def drain():
        for wait in pending:
            wait()

    def go(copy):
        copy.start()
        pending.append(copy.wait_send)

    def z_copy(k, s, src, dst, to):
        return remote(src(s), dst.at[to], zsem.at[k, 0, s], zsem.at[k, 1, to], {"exp": ahead(s)})

    def z_send(k, src, dst, low, high):
        def start(i, _):
            s = high - 1 - i
            z_copy(k, s, src, dst, mirror(s)).start()
            return 0

        def wait(s, _):
            z_copy(k, s, src, dst, s).wait_send()
            return 0

        lax.fori_loop(0, high - low, start, 0)
        pending.append(lambda: lax.fori_loop(low, high, wait, 0))

    def z_wait(k, src, dst, low, high):
        def wait(s, _):
            z_copy(k, s, src, dst, s).wait_recv()
            return 0

        lax.fori_loop(low, high, wait, 0)

    def y_copy(k, group, t, src, dst, mark):
        return remote(
            src, dst, ysem.at[k, group, 0, t], ysem.at[k, group, 1, mark], {"attn": t * 2 + c}
        )

    def g_copy(k, group, i, ref):
        return remote(
            ref, ref, gsem.at[k, group, 0, i], gsem.at[k, group, 1, i], {"attn": y * 2 + other}
        )

    def c_copy(k, n):
        w = pl.ds(n * NC, NC)
        return remote(
            sib_src.at[k, :, w], sib_dst.at[k, :, w], csem.at[k, 0, n], csem.at[k, 1, n],
            {"attn": y * 2 + other},
        )

    def x_copy(k, t, src, dst, mark):
        return remote(src, dst, xsem.at[k, 0, t], xsem.at[k, 1, mark], {"seq": t})

    def ys():
        return [lax.rem(y + d, NY) for d in far_first(NY)]

    def xs():
        return [lax.rem(x + d, S) for d in far_first(S)]

    def block(ref, core, yy, group):
        return ref.at[pl.ds(pl.multiple_of(core * HALF + yy * RB + group * RG, RG), RG)]

    def rows(ref, i):
        return ref.at[pl.ds(pl.multiple_of(i * CH, CH), CH)]

    def z_near(k, blk, buf):
        z_send(k, lambda s: blk, buf, 1, 2 * W + 1)

    def z_far(k, blk, buf):
        z_wait(k, lambda s: blk, buf, 2 * W - 1, 2 * W + 1)
        for j in range(W, 0, -1):
            for at, to, peer in (
                (2 * W, 2 * (W + j) if j < W else E - 1, z + j),
                (2 * W - 1, 2 * (W + j) - 1, z + E - j),
            )[: 2 if j < W else 1]:
                go(
                    remote(
                        buf.at[at], buf.at[to], zsem.at[k, 0, to], zsem.at[k, 1, to],
                        {"exp": lax.rem(peer, E)},
                    )
                )

    z_near(TOK, tok_blk, tok_z)
    z_near(COT, cot_blk, cot_z)
    tok_z[0] = tok_blk[...]
    cot_z[0] = cot_blk[...]
    local[2].wait()
    wide[2 * FT : 3 * FT, :] = gt[...].T
    local[3].wait()
    wide[3 * FT : 4 * FT, :] = ut[...].T

    def assemble(k, group, blk, buf, whole):
        low = group * (E // 2)
        if group == 0:
            z_wait(k, lambda s: blk, buf, 1, 2 * W - 1)
        else:
            z_wait(k, lambda s: blk, buf, 2 * W + 1, E)
        width = blk.shape[1]
        for i in range(E // 2):
            flat[i * R : (i + 1) * R, :width] = buf[low + i].astype(F32)
        mine = block(whole, c, y, group)
        mine[...] = flat[:, :width].astype(BF)
        for t in ys():
            go(y_copy(k, group, t, mine, mine, y))
        go(g_copy(k, group, y, mine))

    def pass_on(k, group, whole):
        for t in reversed(ys()):
            got = block(whole, c, t, group)
            y_copy(k, group, t, got, got, t).wait_recv()
            go(g_copy(k, group, t, got))

    def from_sibling(k, whole):
        for group in range(2):
            for t in range(NY):
                g_copy(k, group, t, block(whole, other, t, group)).wait_recv()

    def half_rows(core):
        return pl.ds(pl.multiple_of(core * HALF, HALF), HALF)

    def project(core):
        r = half_rows(core)
        v = nt(xt[r, :D], wide[...])
        speech = xt[r, D:].astype(F32) < 0.5
        p1[r, 0:FT] = jnp.where(speech, v[:, :FT], v[:, 2 * FT : 3 * FT])
        p1[r, FT : 2 * FT] = jnp.where(speech, v[:, FT : 2 * FT], v[:, 3 * FT : 4 * FT])
        p1[r, 2 * FT :] = v[:, 4 * FT :]

    def x_half(k, core, src, dst):
        for t in xs():

            @pl.when(t // (S // 2) == core)
            def _():
                x_copy(k, t, rows(src, t), dst.at[x], x).start()

    def hidden_grad(core):
        r = half_rows(core)
        speech = xt[r, D:].astype(F32) < 0.5
        v = nt(ct[r, :], down[...])
        near = jnp.where(speech, v[:, :FT], v[:, FT : 2 * FT])
        tail = v[:, 2 * FT :]
        tail = jnp.concatenate([tail, jnp.zeros_like(tail)], axis=1)
        p2[r, 0:FT] = near
        p2[r, FT:] = tail
        p2b[r, 0:FT] = near.astype(BF)
        p2b[r, FT:] = tail.astype(BF)

    z_far(TOK, tok_blk, tok_z)
    assemble(TOK, 0, tok_blk, tok_z, xt)
    z_far(COT, cot_blk, cot_z)
    assemble(TOK, 1, tok_blk, tok_z, xt)
    assemble(COT, 0, cot_blk, cot_z, ct)
    for copy in local[4:]:
        copy.wait()
    pass_on(TOK, 0, xt)
    assemble(COT, 1, cot_blk, cot_z, ct)
    pass_on(TOK, 1, xt)
    project(c)
    x_half(0, c, p1, r1)
    from_sibling(TOK, xt)
    project(other)
    x_half(0, other, p1, r1)
    pass_on(COT, 0, ct)
    pass_on(COT, 1, ct)
    hidden_grad(c)
    x_half(1, c, p2b, r2)
    from_sibling(COT, ct)
    hidden_grad(other)
    x_half(1, other, p2b, r2)
    for t in xs():
        pending.append(x_copy(0, t, rows(p1, t), r1.at[x], x).wait_send)
        pending.append(x_copy(1, t, rows(p2b, t), r2.at[x], x).wait_send)

    def split(v):
        return v[:, :FX], v[:, FX : 2 * FX]

    total = rows(p1, x)[...]
    for t in xs():
        x_copy(0, t, r1.at[t], r1.at[t], t).wait_recv()
        total += r1[t]
    gu[...] = total
    g, u = total[:, :FT], total[:, FT : 2 * FT]
    ge, ue = split(total[:, 2 * FT :])
    he = jax.nn.silu(ge) * ue
    mine = rows(hb, x)
    mine[:, 0:FT] = (jax.nn.silu(g) * u).astype(BF)
    mine[:, FT:] = jnp.concatenate([he, jnp.zeros_like(he)], axis=1).astype(BF)
    for t in xs():
        go(x_copy(2, t, mine, mine, x))

    total = rows(p2, x)[...]
    for t in xs():
        x_copy(1, t, r2.at[t], r2.at[t], t).wait_recv()
        total += r2[t].astype(F32)

    def back(dh, g, u):
        sig = jax.nn.sigmoid(g)
        return dh * u * sig * (1.0 + g * (1.0 - sig)), dh * (g * sig)

    dg, du = back(total[:, :FT], gu[:, :FT], gu[:, FT : 2 * FT])
    ge, ue = split(gu[:, 2 * FT :])
    dge, due = back(total[:, FT : FT + FX], ge, ue)
    mine_g = rows(gb, x)
    mine_g[:, 0:FT] = dg.astype(BF)
    mine_g[:, FT : 2 * FT] = du.astype(BF)
    mine_g[:, 2 * FT :] = jnp.concatenate([dge, due], axis=1).astype(BF)
    for t in xs():
        go(x_copy(3, t, mine_g, mine_g, x))

    def kinds(r):
        text = xt[r, D:]
        return (1.0 - text.astype(F32)).astype(BF), text

    def out_left(core):
        r = half_rows(core)
        speech, text = kinds(r)
        h = hb[r, 0:FT]
        hcat[r, 0:FT] = h * speech
        hcat[r, FT : 2 * FT] = h * text
        hcat[r, 2 * FT :] = hb[r, FT : FT + FX] * speech[:, :FX]
        return hcat[r, :]

    def grad_left(core):
        r = half_rows(core)
        speech, text = kinds(r)
        dg, du = gb[r, 0:FT], gb[r, FT : 2 * FT]
        return jnp.concatenate(
            [dg * speech, du * speech, dg * text, du * text, gb[r, 2 * FT :] * speech], axis=1
        )

    def partials(k, left, weights):
        rows_other = left(other)
        for n in range(D // NC):
            w = slice(n * NC, (n + 1) * NC)
            sib_src[k, :, w] = nn(rows_other, weights[:, w]).astype(BF)
            go(c_copy(k, n))
        rows_own = left(c)
        for n in range(D // NC):
            w = slice(n * NC, (n + 1) * NC)
            acc[k, :, w] = nn(rows_own, weights[:, w])

    def part(ref, k, t, group):
        return ref.at[k, pl.ds(pl.multiple_of(t * RB + group * RG, RG), RG)]

    def over_y(k):
        for n in range(D // NC):
            c_copy(k, n).wait_recv()
        for group in (1, 0):
            for t in ys():
                v = part(acc, k, t, group)[...] + part(sib_dst, k, t, group)[...].astype(F32)
                part(y_src, k, t, group)[...] = v.astype(BF)
                go(y_copy(2 + k, group, t, part(y_src, k, t, group), y_dst.at[k, group, y], y))

    def over_z(k):
        for group in (1, 0):
            total = part(acc, k, y, group)[...] + part(sib_dst, k, y, group)[...].astype(F32)
            for t in reversed(ys()):
                got = y_dst.at[k, group, t]
                y_copy(2 + k, group, t, got, got, t).wait_recv()
                total += got[...].astype(F32)
            low = group * (E // 2)
            for i in range(E // 2):
                z_src[k, low + i] = total[i * R : (i + 1) * R].astype(BF)
            z_send(2 + k, lambda s: z_src.at[k, s], z_dst.at[k], max(low, 1), low + E // 2)
        stores[2 + k].start()

    def down_grads():
        left = hcat[...].T

        def body(n, _):
            w = pl.ds(pl.multiple_of(n * NC, NC), NC)
            v = nn(left, ct[:, w]).astype(BF)
            dsg[0:FT, w] = v[0:FT]
            dtg[:, w] = v[FT : 2 * FT]
            dsg[FT:, w] = v[2 * FT :]
            return 0

        lax.fori_loop(0, D // NC, body, 0)
        stores[0].start()
        stores[1].start()

    for t in xs():
        got = rows(hb, t)
        x_copy(2, t, got, got, t).wait_recv()
    partials(0, out_left, down)
    over_y(0)
    down_grads()
    for t in xs():
        got = rows(gb, t)
        x_copy(3, t, got, got, t).wait_recv()
    partials(1, grad_left, wide)
    over_y(1)
    over_z(0)
    over_z(1)
    for k in range(2):
        z_wait(2 + k, lambda s: z_src.at[k, s], z_dst.at[k], 1, E)

    drain()
    for copy in stores:
        copy.wait()


def place(slots, dsg, dtg, mixed_o, grad_o, dsg_o, dtg_o, slots_v, mixed, grad, dsg_v, dtg_v, sem):
    def copies(src, dst, row):
        strip = 64 if src.shape[0] % 64 == 0 else src.shape[0]
        return [
            pltpu.make_async_copy(src.at[pl.ds(i, strip)], dst.at[pl.ds(i, strip)], sem.at[row, i // strip])
            for i in range(0, src.shape[0], strip)
        ]

    parts = [pltpu.make_async_copy(slots.at[k], slots_v.at[k], sem.at[4, k]) for k in range(2)]
    loads = copies(dsg, dsg_v, 0) + copies(dtg, dtg_v, 1)
    stores = copies(dsg_v, dsg_o, 2) + copies(dtg_v, dtg_o, 3)
    for copy in parts + loads:
        copy.start()
    for load, store in zip(loads, stores):
        load.wait()
        store.start()
    for k, (held, out) in enumerate(((mixed, mixed_o), (grad, grad_o))):
        parts[k].wait()
        total = slots_v[k, 0].astype(F32)
        for i in range(1, slots_v.shape[1]):
            total += slots_v[k, i].astype(F32)
        held[...] = total.astype(BF)
        stores.append(pltpu.make_async_copy(held, out, sem.at[5, k]))
        stores[-1].start()
    for store in stores:
        store.wait()


def shards(NY, E, S, tokens, modality, cotangent, *weights):
    R, D = tokens.shape
    gs, us, ds, gt, ut, dt = weights
    gs, us = gs.T, us.T
    FS, FT = gs.shape[0], gt.shape[1]
    RB = E * R
    HALF = NY * RB
    T = 2 * HALF
    CH = T // S
    DMA = pltpu.SemaphoreType.DMA
    hbm_spec = pl.BlockSpec(memory_space=pltpu.HBM)
    slots = jax.ShapeDtypeStruct((2, E, R, D), BF)
    own = jax.ShapeDtypeStruct((R, D), BF)
    downs = (jax.ShapeDtypeStruct(ds.shape, BF), jax.ShapeDtypeStruct(dt.shape, BF))
    outs = pl.pallas_call(
        functools.partial(kernel, NY, E, S),
        out_shape=(slots, *downs),
        in_specs=[hbm_spec, pl.BlockSpec(memory_space=pltpu.SMEM)] + [hbm_spec] * 7,
        out_specs=[hbm_spec] * 3,
        scratch_shapes=[
            pltpu.VMEM(gt.shape, BF),
            pltpu.VMEM(ut.shape, BF),
            pltpu.VMEM((2 * (FS + FT), D), BF),
            pltpu.VMEM((FS + FT, D), BF),
            pltpu.VMEM((R, D + LANE), BF),
            pltpu.VMEM((R, D), BF),
            pltpu.VMEM((E, R, D + LANE), BF),
            pltpu.VMEM((E, R, D), BF),
            pltpu.VMEM((RB // 2, D + LANE), F32),
            pltpu.VMEM((T, D + LANE), BF),
            pltpu.VMEM((T, D), BF),
            pltpu.VMEM((T, 3 * FT), F32),
            pltpu.VMEM((T, 2 * FT), F32),
            pltpu.VMEM((T, 2 * FT), BF),
            pltpu.VMEM((S, CH, 3 * FT), F32),
            pltpu.VMEM((S, CH, 2 * FT), BF),
            pltpu.VMEM((CH, 3 * FT), F32),
            pltpu.VMEM((T, 2 * FT), BF),
            pltpu.VMEM((T, 3 * FT), BF),
            pltpu.VMEM((2, HALF, D), BF),
            pltpu.VMEM((2, HALF, D), BF),
            pltpu.VMEM((2, HALF, D), F32),
            pltpu.VMEM((2, HALF, D), BF),
            pltpu.VMEM((2, 2, NY, RB // 2, D), BF),
            pltpu.VMEM((2, E, R, D), BF),
            pltpu.VMEM((T, FS + FT), BF),
            pltpu.VMEM(ds.shape, BF),
            pltpu.VMEM(dt.shape, BF),
            DMA((11,)),
            DMA((4,)),
            DMA((4, 2, E)),
            DMA((4, 2, 2, NY)),
            DMA((2, 2, 2, NY)),
            DMA((2, 2, 8)),
            DMA((4, 2, S)),
        ],
        compiler_params=pltpu.CompilerParams(
            collective_id=0, has_side_effects=True, vmem_limit_bytes=62 << 20
        ),
    )(tokens, modality, cotangent, gs, us, ds, gt, ut, dt)
    return pl.pallas_call(
        place,
        out_shape=(own, own, *downs),
        in_specs=[hbm_spec] * 3,
        out_specs=[hbm_spec] * 4,
        scratch_shapes=[pltpu.VMEM(o.shape, BF) for o in (slots, own, own, *downs)] + [DMA((6, 32))],
        compiler_params=pltpu.CompilerParams(vmem_limit_bytes=62 << 20),
    )(*outs)


def solution(mesh):
    NY, E, S = mesh.shape["attn"] // 2, mesh.shape["exp"], mesh.shape["seq"]
    row = P(("attn", "exp"), "seq")
    col = P("seq", ("attn", "exp"))
    return jax.shard_map(
        functools.partial(shards, NY, E, S),
        mesh=mesh,
        in_specs=(row, P(("attn", "exp")), row, col, col, row, col, col, row),
        out_specs=(row, row, row, row),
        check_vma=False,
    )
```

```python
import functools

import jax
import jax.numpy as jnp
from jax import lax
from jax.experimental import pallas as pl
from jax.experimental.pallas import tpu as pltpu
from jax.sharding import PartitionSpec as P

BF = jnp.bfloat16
F32 = jnp.float32
MESH = pl.DeviceIdType.MESH
LANE = 128
TOK, COT = range(2)


def nn(left, right):
    return lax.dot_general(left, right, (((1,), (0,)), ((), ())), preferred_element_type=F32)


def nt(left, right):
    return lax.dot_general(left, right, (((1,), (1,)), ((), ())), preferred_element_type=F32)


def far_first(count):
    return sorted(range(1, count), key=lambda d: -min(d, count - d))


def remote(src, dst, send, recv, device):
    return pltpu.make_async_remote_copy(
        src_ref=src, dst_ref=dst, send_sem=send, recv_sem=recv, device_id=device, device_id_type=MESH
    )


def kernel(
    NY, E, S,
    tok, mod, cot, w_gs, w_us, w_ds, w_gt, w_ut, w_dt,
    mixed_o, grad_o, dsg_o, dtg_o,
    gt, ut, wide, down,
    tok_blk, cot_blk, tok_z, cot_z, xt, ct,
    p1, p2, r1, r2, gu, hb, gb,
    sib_src, sib_dst, acc, y_src, y_dst, z_src, z_dst, hcat, mixed, grad, dsg, dtg,
    wsem, osem, zsem, ysem, gsem, csem, xsem,
):
    attn, z, x = lax.axis_index("attn"), lax.axis_index("exp"), lax.axis_index("seq")
    y, c = attn // 2, attn % 2
    other = 1 - c
    R, D = cot_blk.shape
    RB = E * R
    RG = RB // 2
    HALF = NY * RB
    CH = 2 * HALF // S
    FS, FT = w_gs.shape[0], gt.shape[1]
    FX = FS - FT
    NC = 512 if D % 512 == 0 else D
    W = E // 4

    barrier = pltpu.get_barrier_semaphore()

    def greet(device):
        pl.semaphore_signal(barrier, inc=1, device_id=device, device_id_type=MESH)

    for k in range(W, 0, -1):
        greet({"exp": lax.rem(z + k, E)})
        greet({"exp": lax.rem(z + E - k, E)})
    for d in far_first(NY):
        greet({"attn": lax.rem(y + d, NY) * 2 + c})
    for d in far_first(S):
        greet({"seq": lax.rem(x + d, S)})
    greet({"attn": y * 2 + other})

    def load(src, at, size, dst, to, n):
        return pltpu.make_async_copy(src.at[pl.ds(at, size)], dst.at[pl.ds(to, size)], wsem.at[n])

    local = [
        pltpu.make_async_copy(tok, tok_blk.at[:, pl.ds(0, D)], wsem.at[0]),
        pltpu.make_async_copy(cot, cot_blk, wsem.at[1]),
        pltpu.make_async_copy(w_gt, gt, wsem.at[2]),
        pltpu.make_async_copy(w_ut, ut, wsem.at[3]),
        load(w_gs, 0, FT, wide, 0, 4),
        load(w_us, 0, FT, wide, FT, 5),
        load(w_gs, FT, FX, wide, 4 * FT, 6),
        load(w_us, FT, FX, wide, 4 * FT + FX, 7),
        load(w_ds, 0, FT, down, 0, 8),
        load(w_dt, 0, FT, down, FT, 9),
        load(w_ds, FT, FX, down, 2 * FT, 10),
    ]
    for copy in local:
        copy.start()
    stores = [
        pltpu.make_async_copy(dsg, dsg_o, osem.at[0]),
        pltpu.make_async_copy(dtg, dtg_o, osem.at[1]),
        pltpu.make_async_copy(mixed, mixed_o, osem.at[2]),
        pltpu.make_async_copy(grad, grad_o, osem.at[3]),
    ]

    local[0].wait()
    kind = jnp.concatenate(
        [jnp.full((1, LANE), mod[i].astype(F32), F32) for i in range(R)], axis=0
    )
    tok_blk[:, D:] = kind.astype(BF)
    local[1].wait()
    pl.semaphore_wait(barrier, 2 * W + (NY - 1) + (S - 1) + 1)

    def ahead(s):
        return lax.rem(z + E + (s + 1) // 2 * (2 * (s % 2) - 1), E)

    def mirror(s):
        return jnp.where(s == E - 1, s, s + 2 * (s % 2) - 1)

    pending = []

    def drain():
        for wait in pending:
            wait()

    def go(copy):
        copy.start()
        pending.append(copy.wait_send)

    def z_copy(k, s, src, dst, to):
        return remote(src(s), dst.at[to], zsem.at[k, 0, s], zsem.at[k, 1, to], {"exp": ahead(s)})

    def z_send(k, src, dst, low, high):
        def start(i, _):
            s = high - 1 - i
            z_copy(k, s, src, dst, mirror(s)).start()
            return 0

        def wait(s, _):
            z_copy(k, s, src, dst, s).wait_send()
            return 0

        lax.fori_loop(0, high - low, start, 0)
        pending.append(lambda: lax.fori_loop(low, high, wait, 0))

    def z_wait(k, src, dst, low, high):
        def wait(s, _):
            z_copy(k, s, src, dst, s).wait_recv()
            return 0

        lax.fori_loop(low, high, wait, 0)

    def y_copy(k, group, t, src, dst, mark):
        return remote(
            src, dst, ysem.at[k, group, 0, t], ysem.at[k, group, 1, mark], {"attn": t * 2 + c}
        )

    def g_copy(k, group, i, ref):
        return remote(
            ref, ref, gsem.at[k, group, 0, i], gsem.at[k, group, 1, i], {"attn": y * 2 + other}
        )

    def c_copy(k, n):
        w = pl.ds(n * NC, NC)
        return remote(
            sib_src.at[k, :, w], sib_dst.at[k, :, w], csem.at[k, 0, n], csem.at[k, 1, n],
            {"attn": y * 2 + other},
        )

    def x_copy(k, t, src, dst, mark):
        return remote(src, dst, xsem.at[k, 0, t], xsem.at[k, 1, mark], {"seq": t})

    def ys():
        return [lax.rem(y + d, NY) for d in far_first(NY)]

    def xs():
        return [lax.rem(x + d, S) for d in far_first(S)]

    def block(ref, core, yy, group):
        return ref.at[pl.ds(pl.multiple_of(core * HALF + yy * RB + group * RG, RG), RG)]

    def rows(ref, i):
        return ref.at[pl.ds(pl.multiple_of(i * CH, CH), CH)]

    def z_near(k, blk, buf):
        z_send(k, lambda s: blk, buf, 1, 2 * W + 1)

    def z_far(k, blk, buf):
        z_wait(k, lambda s: blk, buf, 2 * W - 1, 2 * W + 1)
        for j in range(W, 0, -1):
            for at, to, peer in (
                (2 * W, 2 * (W + j) if j < W else E - 1, z + j),
                (2 * W - 1, 2 * (W + j) - 1, z + E - j),
            )[: 2 if j < W else 1]:
                go(
                    remote(
                        buf.at[at], buf.at[to], zsem.at[k, 0, to], zsem.at[k, 1, to],
                        {"exp": lax.rem(peer, E)},
                    )
                )

    z_near(TOK, tok_blk, tok_z)
    z_near(COT, cot_blk, cot_z)
    tok_z[0] = tok_blk[...]
    cot_z[0] = cot_blk[...]
    local[2].wait()
    wide[2 * FT : 3 * FT, :] = gt[...].T
    local[3].wait()
    wide[3 * FT : 4 * FT, :] = ut[...].T

    def assemble(k, group, blk, buf, whole):
        low = group * (E // 2)
        if group == 0:
            z_wait(k, lambda s: blk, buf, 1, 2 * W - 1)
        else:
            z_wait(k, lambda s: blk, buf, 2 * W + 1, E)
        width = blk.shape[1]
        mine = block(whole, c, y, group)
        mine[...] = jnp.concatenate(
            [buf[low + i].astype(F32) for i in range(E // 2)], axis=0
        ).astype(BF)
        for t in ys():
            go(y_copy(k, group, t, mine, mine, y))
        go(g_copy(k, group, y, mine))

    def pass_on(k, group, whole):
        for t in reversed(ys()):
            got = block(whole, c, t, group)
            y_copy(k, group, t, got, got, t).wait_recv()
            go(g_copy(k, group, t, got))

    def from_sibling(k, whole):
        for group in range(2):
            for t in range(NY):
                g_copy(k, group, t, block(whole, other, t, group)).wait_recv()

    def half_rows(core):
        return pl.ds(pl.multiple_of(core * HALF, HALF), HALF)

    def project(core):
        r = half_rows(core)
        v = nt(xt[r, :D], wide[...])
        speech = xt[r, D:].astype(F32) < 0.5
        p1[r, 0:FT] = jnp.where(speech, v[:, :FT], v[:, 2 * FT : 3 * FT])
        p1[r, FT : 2 * FT] = jnp.where(speech, v[:, FT : 2 * FT], v[:, 3 * FT : 4 * FT])
        p1[r, 2 * FT :] = v[:, 4 * FT :]

    def x_half(k, core, src, dst):
        for t in xs():

            @pl.when(t // (S // 2) == core)
            def _():
                x_copy(k, t, rows(src, t), dst.at[x], x).start()

    def hidden_grad(core):
        r = half_rows(core)
        speech = xt[r, D:].astype(F32) < 0.5
        v = nt(ct[r, :], down[...])
        near = jnp.where(speech, v[:, :FT], v[:, FT : 2 * FT])
        tail = v[:, 2 * FT :]
        tail = jnp.concatenate([tail, jnp.zeros_like(tail)], axis=1)
        p2[r, 0:FT] = near
        p2[r, FT:] = tail

    z_far(TOK, tok_blk, tok_z)
    z_far(COT, cot_blk, cot_z)
    assemble(TOK, 0, tok_blk, tok_z, xt)
    assemble(TOK, 1, tok_blk, tok_z, xt)
    assemble(COT, 0, cot_blk, cot_z, ct)
    for copy in local[4:]:
        copy.wait()
    pass_on(TOK, 0, xt)
    assemble(COT, 1, cot_blk, cot_z, ct)
    pass_on(TOK, 1, xt)
    project(c)
    x_half(0, c, p1, r1)
    from_sibling(TOK, xt)
    project(other)
    x_half(0, other, p1, r1)
    pass_on(COT, 0, ct)
    pass_on(COT, 1, ct)
    hidden_grad(c)
    x_half(1, c, p2, r2)
    from_sibling(COT, ct)
    hidden_grad(other)
    x_half(1, other, p2, r2)
    for t in xs():
        pending.append(x_copy(0, t, rows(p1, t), r1.at[x], x).wait_send)
        pending.append(x_copy(1, t, rows(p2, t), r2.at[x], x).wait_send)

    def split(v):
        return v[:, :FX], v[:, FX : 2 * FX]

    total = rows(p1, x)[...]
    for t in xs():
        x_copy(0, t, r1.at[t], r1.at[t], t).wait_recv()
        total += r1[t]
    gu[...] = total
    g, u = total[:, :FT], total[:, FT : 2 * FT]
    ge, ue = split(total[:, 2 * FT :])
    he = jax.nn.silu(ge) * ue
    mine = rows(hb, x)
    mine[:, 0:FT] = (jax.nn.silu(g) * u).astype(BF)
    mine[:, FT:] = jnp.concatenate([he, jnp.zeros_like(he)], axis=1).astype(BF)
    for t in xs():
        go(x_copy(2, t, mine, mine, x))

    total = rows(p2, x)[...]
    for t in xs():
        x_copy(1, t, r2.at[t], r2.at[t], t).wait_recv()
        total += r2[t]

    def back(dh, g, u):
        sig = jax.nn.sigmoid(g)
        return dh * u * sig * (1.0 + g * (1.0 - sig)), dh * (g * sig)

    dg, du = back(total[:, :FT], gu[:, :FT], gu[:, FT : 2 * FT])
    ge, ue = split(gu[:, 2 * FT :])
    dge, due = back(total[:, FT : FT + FX], ge, ue)
    mine_g = rows(gb, x)
    mine_g[:, 0:FT] = dg.astype(BF)
    mine_g[:, FT : 2 * FT] = du.astype(BF)
    mine_g[:, 2 * FT :] = jnp.concatenate([dge, due], axis=1).astype(BF)
    for t in xs():
        go(x_copy(3, t, mine_g, mine_g, x))

    def kinds(r):
        text = xt[r, D:]
        return (1.0 - text.astype(F32)).astype(BF), text

    def out_left(core):
        r = half_rows(core)
        speech, text = kinds(r)
        h = hb[r, 0:FT]
        hcat[r, 0:FT] = h * speech
        hcat[r, FT : 2 * FT] = h * text
        hcat[r, 2 * FT :] = hb[r, FT : FT + FX] * speech[:, :FX]
        return hcat[r, :]

    def grad_left(core):
        r = half_rows(core)
        speech, text = kinds(r)
        dg, du = gb[r, 0:FT], gb[r, FT : 2 * FT]
        return jnp.concatenate(
            [dg * speech, du * speech, dg * text, du * text, gb[r, 2 * FT :] * speech], axis=1
        )

    def partials(k, left, weights):
        rows_other = left(other)
        for n in range(D // NC):
            w = slice(n * NC, (n + 1) * NC)
            sib_src[k, :, w] = nn(rows_other, weights[:, w]).astype(BF)
            go(c_copy(k, n))
        rows_own = left(c)
        for n in range(D // NC):
            w = slice(n * NC, (n + 1) * NC)
            acc[k, :, w] = nn(rows_own, weights[:, w])

    def part(ref, k, t, group):
        return ref.at[k, pl.ds(pl.multiple_of(t * RB + group * RG, RG), RG)]

    def over_y(k):
        for n in range(D // NC):
            c_copy(k, n).wait_recv()
        for group in (1, 0):
            for t in ys():
                v = part(acc, k, t, group)[...] + part(sib_dst, k, t, group)[...].astype(F32)
                part(y_src, k, t, group)[...] = v.astype(BF)
                go(y_copy(2 + k, group, t, part(y_src, k, t, group), y_dst.at[k, group, y], y))

    def over_z(k):
        for group in (1, 0):
            total = part(acc, k, y, group)[...] + part(sib_dst, k, y, group)[...].astype(F32)
            for t in reversed(ys()):
                got = y_dst.at[k, group, t]
                y_copy(2 + k, group, t, got, got, t).wait_recv()
                total += got[...].astype(F32)
            low = group * (E // 2)
            for i in range(E // 2):
                z_src[k, low + i] = total[i * R : (i + 1) * R].astype(BF)
            z_send(2 + k, lambda s: z_src.at[k, s], z_dst.at[k], max(low, 1), low + E // 2)

    def finish(k, out):
        z_wait(2 + k, lambda s: z_src.at[k, s], z_dst.at[k], 1, E)
        total = z_src[k, 0].astype(F32)
        for i in range(1, E):
            total += z_dst[k, i].astype(F32)
        out[...] = total.astype(BF)

    def down_grads():
        left = hcat[...].T

        def body(n, _):
            w = pl.ds(pl.multiple_of(n * NC, NC), NC)
            v = nn(left, ct[:, w]).astype(BF)
            dsg[0:FT, w] = v[0:FT]
            dtg[:, w] = v[FT : 2 * FT]
            dsg[FT:, w] = v[2 * FT :]
            return 0

        lax.fori_loop(0, D // NC, body, 0)
        stores[0].start()
        stores[1].start()

    for t in xs():
        got = rows(hb, t)
        x_copy(2, t, got, got, t).wait_recv()
    partials(0, out_left, down)
    over_y(0)
    down_grads()
    for t in xs():
        got = rows(gb, t)
        x_copy(3, t, got, got, t).wait_recv()
    partials(1, grad_left, wide)
    over_y(1)
    over_z(0)
    over_z(1)
    finish(0, mixed)
    stores[2].start()
    finish(1, grad)
    stores[3].start()

    drain()
    for copy in stores:
        copy.wait()


def place(*refs):
    hold, sem = refs[8:12], refs[12]
    loads, stores = [], []
    for src, dst, mid in zip(refs[:4], refs[4:8], hold):
        strip = 64 if src.shape[0] % 64 == 0 else src.shape[0]
        for i in range(0, src.shape[0], strip):
            part, n = pl.ds(i, strip), len(loads)
            loads.append(pltpu.make_async_copy(src.at[part], mid.at[part], sem.at[0, n]))
            stores.append(pltpu.make_async_copy(mid.at[part], dst.at[part], sem.at[1, n]))
    for load in loads:
        load.start()
    for load, store in zip(loads, stores):
        load.wait()
        store.start()
    for store in stores:
        store.wait()


def shards(NY, E, S, tokens, modality, cotangent, *weights):
    R, D = tokens.shape
    gs, us, ds, gt, ut, dt = weights
    gs, us = gs.T, us.T
    FS, FT = gs.shape[0], gt.shape[1]
    RB = E * R
    HALF = NY * RB
    T = 2 * HALF
    CH = T // S
    DMA = pltpu.SemaphoreType.DMA
    hbm_spec = pl.BlockSpec(memory_space=pltpu.HBM)
    out_shape = (
        jax.ShapeDtypeStruct((R, D), BF),
        jax.ShapeDtypeStruct((R, D), BF),
        jax.ShapeDtypeStruct(ds.shape, BF),
        jax.ShapeDtypeStruct(dt.shape, BF),
    )
    outs = pl.pallas_call(
        functools.partial(kernel, NY, E, S),
        out_shape=out_shape,
        in_specs=[hbm_spec, pl.BlockSpec(memory_space=pltpu.SMEM)] + [hbm_spec] * 7,
        out_specs=[hbm_spec] * 4,
        scratch_shapes=[
            pltpu.VMEM(gt.shape, BF),
            pltpu.VMEM(ut.shape, BF),
            pltpu.VMEM((2 * (FS + FT), D), BF),
            pltpu.VMEM((FS + FT, D), BF),
            pltpu.VMEM((R, D + LANE), BF),
            pltpu.VMEM((R, D), BF),
            pltpu.VMEM((E, R, D + LANE), BF),
            pltpu.VMEM((E, R, D), BF),
            pltpu.VMEM((T, D + LANE), BF),
            pltpu.VMEM((T, D), BF),
            pltpu.VMEM((T, 3 * FT), F32),
            pltpu.VMEM((T, 2 * FT), F32),
            pltpu.VMEM((S, CH, 3 * FT), F32),
            pltpu.VMEM((S, CH, 2 * FT), F32),
            pltpu.VMEM((CH, 3 * FT), F32),
            pltpu.VMEM((T, 2 * FT), BF),
            pltpu.VMEM((T, 3 * FT), BF),
            pltpu.VMEM((2, HALF, D), BF),
            pltpu.VMEM((2, HALF, D), BF),
            pltpu.VMEM((2, HALF, D), F32),
            pltpu.VMEM((2, HALF, D), BF),
            pltpu.VMEM((2, 2, NY, RB // 2, D), BF),
            pltpu.VMEM((2, E, R, D), BF),
            pltpu.VMEM((2, E, R, D), BF),
            pltpu.VMEM((T, FS + FT), BF),
            pltpu.VMEM((R, D), BF),
            pltpu.VMEM((R, D), BF),
            pltpu.VMEM(ds.shape, BF),
            pltpu.VMEM(dt.shape, BF),
            DMA((11,)),
            DMA((4,)),
            DMA((4, 2, E)),
            DMA((4, 2, 2, NY)),
            DMA((2, 2, 2, NY)),
            DMA((2, 2, 8)),
            DMA((4, 2, S)),
        ],
        compiler_params=pltpu.CompilerParams(
            collective_id=0, has_side_effects=True, vmem_limit_bytes=62 << 20
        ),
    )(tokens, modality, cotangent, gs, us, ds, gt, ut, dt)
    return pl.pallas_call(
        place,
        out_shape=out_shape,
        in_specs=[hbm_spec] * 4,
        out_specs=[hbm_spec] * 4,
        scratch_shapes=[pltpu.VMEM(o.shape, BF) for o in out_shape] + [DMA((2, 16))],
        compiler_params=pltpu.CompilerParams(vmem_limit_bytes=62 << 20),
    )(*outs)


def solution(mesh):
    NY, E, S = mesh.shape["attn"] // 2, mesh.shape["exp"], mesh.shape["seq"]
    row = P(("attn", "exp"), "seq")
    col = P("seq", ("attn", "exp"))
    return jax.shard_map(
        functools.partial(shards, NY, E, S),
        mesh=mesh,
        in_specs=(row, P(("attn", "exp")), row, col, col, row, col, col, row),
        out_specs=(row, row, row, row),
        check_vma=False,
    )
```

```python
import functools

import jax
import jax.numpy as jnp
from jax import lax
from jax.experimental import pallas as pl
from jax.experimental.pallas import tpu as pltpu
from jax.sharding import PartitionSpec as P

BF = jnp.bfloat16
F32 = jnp.float32
MESH = pl.DeviceIdType.MESH
LANE = 128
TOK, COT = range(2)


def nn(left, right):
    return lax.dot_general(left, right, (((1,), (0,)), ((), ())), preferred_element_type=F32)


def nt(left, right):
    return lax.dot_general(left, right, (((1,), (1,)), ((), ())), preferred_element_type=F32)


def far_first(count):
    return sorted(range(1, count), key=lambda d: -min(d, count - d))


def remote(src, dst, send, recv, device):
    return pltpu.make_async_remote_copy(
        src_ref=src, dst_ref=dst, send_sem=send, recv_sem=recv, device_id=device, device_id_type=MESH
    )


def kernel(
    NY, E, S,
    tok, mod, cot, w_gs, w_us, w_ds, w_gt, w_ut, w_dt,
    mixed, grad, dsg, dtg,
    gt, ut, wide, down,
    tok_blk, cot_blk, tok_z, cot_z, xt, ct,
    p1, p2, r1, r2, gu, hb, gb,
    sib_src, sib_dst, acc, y_src, y_dst, z_src, z_dst, hcat,
    wsem, zsem, ysem, gsem, csem, xsem,
):
    attn, z, x = lax.axis_index("attn"), lax.axis_index("exp"), lax.axis_index("seq")
    y, c = attn // 2, attn % 2
    other = 1 - c
    R, D = cot_blk.shape
    RB = E * R
    RG = RB // 2
    HALF = NY * RB
    CH = 2 * HALF // S
    FS, FT = w_gs.shape[0], gt.shape[1]
    FX = FS - FT
    NC = 512 if D % 512 == 0 else D
    W = E // 4

    barrier = pltpu.get_barrier_semaphore()

    def greet(device):
        pl.semaphore_signal(barrier, inc=1, device_id=device, device_id_type=MESH)

    for k in range(W, 0, -1):
        greet({"exp": lax.rem(z + k, E)})
        greet({"exp": lax.rem(z + E - k, E)})
    for d in far_first(NY):
        greet({"attn": lax.rem(y + d, NY) * 2 + c})
    for d in far_first(S):
        greet({"seq": lax.rem(x + d, S)})
    greet({"attn": y * 2 + other})

    def load(src, at, size, dst, to, n):
        return pltpu.make_async_copy(src.at[pl.ds(at, size)], dst.at[pl.ds(to, size)], wsem.at[n])

    local = [
        pltpu.make_async_copy(tok, tok_blk.at[:, pl.ds(0, D)], wsem.at[0]),
        pltpu.make_async_copy(cot, cot_blk, wsem.at[1]),
        pltpu.make_async_copy(w_gt, gt, wsem.at[2]),
        pltpu.make_async_copy(w_ut, ut, wsem.at[3]),
        load(w_gs, 0, FT, wide, 0, 4),
        load(w_us, 0, FT, wide, FT, 5),
        load(w_gs, FT, FX, wide, 4 * FT, 6),
        load(w_us, FT, FX, wide, 4 * FT + FX, 7),
        load(w_ds, 0, FT, down, 0, 8),
        load(w_dt, 0, FT, down, FT, 9),
        load(w_ds, FT, FX, down, 2 * FT, 10),
    ]
    for copy in local:
        copy.start()

    local[0].wait()
    kind = jnp.concatenate(
        [jnp.full((1, LANE), mod[i].astype(F32), F32) for i in range(R)], axis=0
    )
    tok_blk[:, D:] = kind.astype(BF)
    local[1].wait()
    pl.semaphore_wait(barrier, 2 * W + (NY - 1) + (S - 1) + 1)

    def ahead(s):
        return lax.rem(z + E + (s + 1) // 2 * (2 * (s % 2) - 1), E)

    def mirror(s):
        return jnp.where(s == E - 1, s, s + 2 * (s % 2) - 1)

    pending = []

    def drain(keep=0):
        while len(pending) > keep:
            pending.pop(0)()

    def go(copy):
        copy.start()
        pending.append(copy.wait_send)

    def z_copy(k, s, src, dst, to):
        return remote(src(s), dst.at[to], zsem.at[k, 0, s], zsem.at[k, 1, to], {"exp": ahead(s)})

    def z_send(k, src, dst, low, high):
        def start(i, _):
            s = high - 1 - i
            z_copy(k, s, src, dst, mirror(s)).start()
            return 0

        def wait(s, _):
            z_copy(k, s, src, dst, s).wait_send()
            return 0

        lax.fori_loop(0, high - low, start, 0)
        pending.append(lambda: lax.fori_loop(low, high, wait, 0))

    def z_wait(k, src, dst, low, high):
        def wait(s, _):
            z_copy(k, s, src, dst, s).wait_recv()
            return 0

        lax.fori_loop(low, high, wait, 0)

    def y_copy(k, group, t, src, dst, mark):
        return remote(
            src, dst, ysem.at[k, group, 0, t], ysem.at[k, group, 1, mark], {"attn": t * 2 + c}
        )

    def g_copy(k, group, i, ref):
        return remote(
            ref, ref, gsem.at[k, group, 0, i], gsem.at[k, group, 1, i], {"attn": y * 2 + other}
        )

    def c_copy(k, n):
        w = pl.ds(n * NC, NC)
        return remote(
            sib_src.at[k, :, w], sib_dst.at[k, :, w], csem.at[k, 0, n], csem.at[k, 1, n],
            {"attn": y * 2 + other},
        )

    def x_copy(k, t, src, dst, mark):
        return remote(src, dst, xsem.at[k, 0, t], xsem.at[k, 1, mark], {"seq": t})

    def ys():
        return [lax.rem(y + d, NY) for d in far_first(NY)]

    def xs():
        return [lax.rem(x + d, S) for d in far_first(S)]

    def block(ref, core, yy, group):
        return ref.at[pl.ds(pl.multiple_of(core * HALF + yy * RB + group * RG, RG), RG)]

    def rows(ref, i):
        return ref.at[pl.ds(pl.multiple_of(i * CH, CH), CH)]

    def z_near(k, blk, buf):
        z_send(k, lambda s: blk, buf, 1, 2 * W + 1)

    def z_far(k, blk, buf):
        z_wait(k, lambda s: blk, buf, 2 * W - 1, 2 * W + 1)
        for j in range(W, 0, -1):
            for at, to, peer in (
                (2 * W, 2 * (W + j) if j < W else E - 1, z + j),
                (2 * W - 1, 2 * (W + j) - 1, z + E - j),
            )[: 2 if j < W else 1]:
                go(
                    remote(
                        buf.at[at], buf.at[to], zsem.at[k, 0, to], zsem.at[k, 1, to],
                        {"exp": lax.rem(peer, E)},
                    )
                )

    z_near(TOK, tok_blk, tok_z)
    z_near(COT, cot_blk, cot_z)
    tok_z[0] = tok_blk[...]
    cot_z[0] = cot_blk[...]
    local[2].wait()
    wide[2 * FT : 3 * FT, :] = gt[...].T
    local[3].wait()
    wide[3 * FT : 4 * FT, :] = ut[...].T

    def assemble(k, group, blk, buf, whole):
        low = group * (E // 2)
        if group == 0:
            z_wait(k, lambda s: blk, buf, 1, 2 * W - 1)
        else:
            z_wait(k, lambda s: blk, buf, 2 * W + 1, E)
        width = blk.shape[1]
        mine = block(whole, c, y, group)
        mine[...] = jnp.concatenate(
            [buf[low + i].astype(F32) for i in range(E // 2)], axis=0
        ).astype(BF)
        for t in ys():
            go(y_copy(k, group, t, mine, mine, y))
        go(g_copy(k, group, y, mine))

    def pass_on(k, group, whole):
        for t in reversed(ys()):
            got = block(whole, c, t, group)
            y_copy(k, group, t, got, got, t).wait_recv()
            go(g_copy(k, group, t, got))

    def from_sibling(k, whole):
        for group in range(2):
            for t in range(NY):
                g_copy(k, group, t, block(whole, other, t, group)).wait_recv()

    def half_rows(core):
        return pl.ds(pl.multiple_of(core * HALF, HALF), HALF)

    def project(core):
        r = half_rows(core)
        v = nt(xt[r, :D], wide[...])
        speech = xt[r, D:].astype(F32) < 0.5
        p1[r, 0:FT] = jnp.where(speech, v[:, :FT], v[:, 2 * FT : 3 * FT])
        p1[r, FT : 2 * FT] = jnp.where(speech, v[:, FT : 2 * FT], v[:, 3 * FT : 4 * FT])
        p1[r, 2 * FT :] = v[:, 4 * FT :]

    def x_half(k, core, src, dst):
        for t in xs():

            @pl.when(t // (S // 2) == core)
            def _():
                x_copy(k, t, rows(src, t), dst.at[x], x).start()

    def hidden_grad(core):
        r = half_rows(core)
        speech = xt[r, D:].astype(F32) < 0.5
        v = nt(ct[r, :], down[...])
        near = jnp.where(speech, v[:, :FT], v[:, FT : 2 * FT])
        tail = v[:, 2 * FT :]
        tail = jnp.concatenate([tail, jnp.zeros_like(tail)], axis=1)
        p2[r, 0:FT] = near
        p2[r, FT:] = tail

    z_far(TOK, tok_blk, tok_z)
    z_far(COT, cot_blk, cot_z)
    assemble(TOK, 0, tok_blk, tok_z, xt)
    assemble(TOK, 1, tok_blk, tok_z, xt)
    assemble(COT, 0, cot_blk, cot_z, ct)
    for copy in local[4:]:
        copy.wait()
    pass_on(TOK, 0, xt)
    assemble(COT, 1, cot_blk, cot_z, ct)
    pass_on(TOK, 1, xt)
    project(c)
    x_half(0, c, p1, r1)
    from_sibling(TOK, xt)
    project(other)
    x_half(0, other, p1, r1)
    pass_on(COT, 0, ct)
    pass_on(COT, 1, ct)
    hidden_grad(c)
    x_half(1, c, p2, r2)
    from_sibling(COT, ct)
    hidden_grad(other)
    x_half(1, other, p2, r2)
    for t in xs():
        pending.append(x_copy(0, t, rows(p1, t), r1.at[x], x).wait_send)
        pending.append(x_copy(1, t, rows(p2, t), r2.at[x], x).wait_send)

    def split(v):
        return v[:, :FX], v[:, FX : 2 * FX]

    total = rows(p1, x)[...]
    for t in xs():
        x_copy(0, t, r1.at[t], r1.at[t], t).wait_recv()
        total += r1[t]
    gu[...] = total
    g, u = total[:, :FT], total[:, FT : 2 * FT]
    ge, ue = split(total[:, 2 * FT :])
    he = jax.nn.silu(ge) * ue
    mine = rows(hb, x)
    mine[:, 0:FT] = (jax.nn.silu(g) * u).astype(BF)
    mine[:, FT:] = jnp.concatenate([he, jnp.zeros_like(he)], axis=1).astype(BF)
    for t in xs():
        go(x_copy(2, t, mine, mine, x))

    total = rows(p2, x)[...]
    for t in xs():
        x_copy(1, t, r2.at[t], r2.at[t], t).wait_recv()
        total += r2[t]

    def back(dh, g, u):
        sig = jax.nn.sigmoid(g)
        return dh * u * sig * (1.0 + g * (1.0 - sig)), dh * (g * sig)

    dg, du = back(total[:, :FT], gu[:, :FT], gu[:, FT : 2 * FT])
    ge, ue = split(gu[:, 2 * FT :])
    dge, due = back(total[:, FT : FT + FX], ge, ue)
    mine_g = rows(gb, x)
    mine_g[:, 0:FT] = dg.astype(BF)
    mine_g[:, FT : 2 * FT] = du.astype(BF)
    mine_g[:, 2 * FT :] = jnp.concatenate([dge, due], axis=1).astype(BF)
    for t in xs():
        go(x_copy(3, t, mine_g, mine_g, x))

    def kinds(r):
        text = xt[r, D:]
        return (1.0 - text.astype(F32)).astype(BF), text

    def out_left(core):
        r = half_rows(core)
        speech, text = kinds(r)
        h = hb[r, 0:FT]
        hcat[r, 0:FT] = h * speech
        hcat[r, FT : 2 * FT] = h * text
        hcat[r, 2 * FT :] = hb[r, FT : FT + FX] * speech[:, :FX]
        return hcat[r, :]

    def grad_left(core):
        r = half_rows(core)
        speech, text = kinds(r)
        dg, du = gb[r, 0:FT], gb[r, FT : 2 * FT]
        return jnp.concatenate(
            [dg * speech, du * speech, dg * text, du * text, gb[r, 2 * FT :] * speech], axis=1
        )

    def partials(k, left, weights):
        rows_other = left(other)
        for n in range(D // NC):
            w = slice(n * NC, (n + 1) * NC)
            sib_src[k, :, w] = nn(rows_other, weights[:, w]).astype(BF)
            go(c_copy(k, n))
        rows_own = left(c)
        for n in range(D // NC):
            w = slice(n * NC, (n + 1) * NC)
            acc[k, :, w] = nn(rows_own, weights[:, w])

    def part(ref, k, t, group):
        return ref.at[k, pl.ds(pl.multiple_of(t * RB + group * RG, RG), RG)]

    def over_y(k):
        for n in range(D // NC):
            c_copy(k, n).wait_recv()
        for group in (1, 0):
            for t in ys():
                v = part(acc, k, t, group)[...] + part(sib_dst, k, t, group)[...].astype(F32)
                part(y_src, k, t, group)[...] = v.astype(BF)
                go(y_copy(2 + k, group, t, part(y_src, k, t, group), y_dst.at[k, group, y], y))

    def over_z(k):
        for group in (1, 0):
            total = part(acc, k, y, group)[...] + part(sib_dst, k, y, group)[...].astype(F32)
            for t in reversed(ys()):
                got = y_dst.at[k, group, t]
                y_copy(2 + k, group, t, got, got, t).wait_recv()
                total += got[...].astype(F32)
            low = group * (E // 2)
            for i in range(E // 2):
                z_src[k, low + i] = total[i * R : (i + 1) * R].astype(BF)
            z_send(2 + k, lambda s: z_src.at[k, s], z_dst.at[k], max(low, 1), low + E // 2)

    def finish(k, out):
        z_wait(2 + k, lambda s: z_src.at[k, s], z_dst.at[k], 1, E)
        total = z_src[k, 0].astype(F32)
        for i in range(1, E):
            total += z_dst[k, i].astype(F32)
        out[...] = total.astype(BF)

    def down_grads():
        left = hcat[...].T

        def body(n, _):
            w = pl.ds(pl.multiple_of(n * NC, NC), NC)
            v = nn(left, ct[:, w]).astype(BF)
            dsg[0:FT, w] = v[0:FT]
            dtg[:, w] = v[FT : 2 * FT]
            dsg[FT:, w] = v[2 * FT :]
            return 0

        lax.fori_loop(0, D // NC, body, 0)

    for t in xs():
        got = rows(hb, t)
        x_copy(2, t, got, got, t).wait_recv()
    partials(0, out_left, down)
    before = len(pending)
    over_y(0)
    sent_y = len(pending) - before + D // NC
    down_grads()
    for t in xs():
        got = rows(gb, t)
        x_copy(3, t, got, got, t).wait_recv()
    partials(1, grad_left, wide)
    before = len(pending)
    over_y(1)
    drain(len(pending) - before + sent_y)
    over_z(0)
    over_z(1)
    drain(2)
    finish(0, mixed)
    drain()
    finish(1, grad)

    drain()


def place(*refs):
    sem, copies = refs[8], []
    for src, dst in zip(refs[:4], refs[4:8]):
        strip = 64 if src.shape[0] % 64 == 0 else src.shape[0]
        for i in range(0, src.shape[0], strip):
            part = pl.ds(i, strip)
            copies.append(pltpu.make_async_copy(src.at[part], dst.at[part], sem.at[len(copies)]))
    for copy in copies:
        copy.start()
    for copy in copies:
        copy.wait()


def shards(NY, E, S, tokens, modality, cotangent, *weights):
    R, D = tokens.shape
    gs, us, ds, gt, ut, dt = weights
    gs, us = gs.T, us.T
    FS, FT = gs.shape[0], gt.shape[1]
    RB = E * R
    HALF = NY * RB
    T = 2 * HALF
    CH = T // S
    DMA = pltpu.SemaphoreType.DMA
    hbm_spec = pl.BlockSpec(memory_space=pltpu.HBM)
    vmem_spec = pl.BlockSpec(memory_space=pltpu.VMEM)
    out_shape = (
        jax.ShapeDtypeStruct((R, D), BF),
        jax.ShapeDtypeStruct((R, D), BF),
        jax.ShapeDtypeStruct(ds.shape, BF),
        jax.ShapeDtypeStruct(dt.shape, BF),
    )
    outs = pl.pallas_call(
        functools.partial(kernel, NY, E, S),
        out_shape=tuple(pltpu.VMEM(o.shape, BF) for o in out_shape),
        in_specs=[hbm_spec, pl.BlockSpec(memory_space=pltpu.SMEM)] + [hbm_spec] * 7,
        out_specs=[vmem_spec] * 4,
        scratch_shapes=[
            pltpu.VMEM(gt.shape, BF),
            pltpu.VMEM(ut.shape, BF),
            pltpu.VMEM((2 * (FS + FT), D), BF),
            pltpu.VMEM((FS + FT, D), BF),
            pltpu.VMEM((R, D + LANE), BF),
            pltpu.VMEM((R, D), BF),
            pltpu.VMEM((E, R, D + LANE), BF),
            pltpu.VMEM((E, R, D), BF),
            pltpu.VMEM((T, D + LANE), BF),
            pltpu.VMEM((T, D), BF),
            pltpu.VMEM((T, 3 * FT), F32),
            pltpu.VMEM((T, 2 * FT), F32),
            pltpu.VMEM((S, CH, 3 * FT), F32),
            pltpu.VMEM((S, CH, 2 * FT), F32),
            pltpu.VMEM((CH, 3 * FT), F32),
            pltpu.VMEM((T, 2 * FT), BF),
            pltpu.VMEM((T, 3 * FT), BF),
            pltpu.VMEM((2, HALF, D), BF),
            pltpu.VMEM((2, HALF, D), BF),
            pltpu.VMEM((2, HALF, D), F32),
            pltpu.VMEM((2, HALF, D), BF),
            pltpu.VMEM((2, 2, NY, RB // 2, D), BF),
            pltpu.VMEM((2, E, R, D), BF),
            pltpu.VMEM((2, E, R, D), BF),
            pltpu.VMEM((T, FS + FT), BF),
            DMA((11,)),
            DMA((4, 2, E)),
            DMA((4, 2, 2, NY)),
            DMA((2, 2, 2, NY)),
            DMA((2, 2, 8)),
            DMA((4, 2, S)),
        ],
        compiler_params=pltpu.CompilerParams(
            collective_id=0, has_side_effects=True, vmem_limit_bytes=58 << 20
        ),
    )(tokens, modality, cotangent, gs, us, ds, gt, ut, dt)
    return pl.pallas_call(
        place,
        out_shape=out_shape,
        in_specs=[vmem_spec] * 4,
        out_specs=[hbm_spec] * 4,
        scratch_shapes=[DMA((16,))],
        compiler_params=pltpu.CompilerParams(vmem_limit_bytes=16 << 20),
    )(*outs)


def solution(mesh):
    NY, E, S = mesh.shape["attn"] // 2, mesh.shape["exp"], mesh.shape["seq"]
    row = P(("attn", "exp"), "seq")
    col = P("seq", ("attn", "exp"))
    return jax.shard_map(
        functools.partial(shards, NY, E, S),
        mesh=mesh,
        in_specs=(row, P(("attn", "exp")), row, col, col, row, col, col, row),
        out_specs=(row, row, row, row),
        check_vma=False,
    )
```

```python
import functools

import jax
import jax.numpy as jnp
from jax import lax
from jax.experimental import pallas as pl
from jax.experimental.pallas import tpu as pltpu
from jax.sharding import PartitionSpec as P

BF = jnp.bfloat16
F32 = jnp.float32
MESH = pl.DeviceIdType.MESH
LANE = 128
TOK, COT = range(2)


def nn(left, right):
    return lax.dot_general(left, right, (((1,), (0,)), ((), ())), preferred_element_type=F32)


def nt(left, right):
    return lax.dot_general(left, right, (((1,), (1,)), ((), ())), preferred_element_type=F32)


def far_first(count):
    return sorted(range(1, count), key=lambda d: -min(d, count - d))


def remote(src, dst, send, recv, device):
    return pltpu.make_async_remote_copy(
        src_ref=src, dst_ref=dst, send_sem=send, recv_sem=recv, device_id=device, device_id_type=MESH
    )


def kernel(
    NY, E, S,
    tok, mod, cot, w_gs, w_us, w_ds, w_gt, w_ut, w_dt,
    mixed, grad, dsg, dtg,
    gt, ut, wide, down,
    tok_blk, cot_blk, tok_z, cot_z, xt, ct,
    p1, p2, r1, r2, gu, hb, gb,
    sib_src, sib_dst, acc, y_src, y_dst, z_src, z_dst, hcat,
    wsem, zsem, ysem, gsem, csem, xsem,
):
    attn, z, x = lax.axis_index("attn"), lax.axis_index("exp"), lax.axis_index("seq")
    y, c = attn // 2, attn % 2
    other = 1 - c
    R, D = cot_blk.shape
    RB = E * R
    RG = RB // 2
    HALF = NY * RB
    CH = 2 * HALF // S
    FS, FT = w_gs.shape[0], gt.shape[1]
    FX = FS - FT
    NC = 512 if D % 512 == 0 else D
    W = E // 4

    barrier = pltpu.get_barrier_semaphore()

    def greet(device):
        pl.semaphore_signal(barrier, inc=1, device_id=device, device_id_type=MESH)

    for k in range(W, 0, -1):
        greet({"exp": lax.rem(z + k, E)})
        greet({"exp": lax.rem(z + E - k, E)})
    for d in far_first(NY):
        greet({"attn": lax.rem(y + d, NY) * 2 + c})
    for d in far_first(S):
        greet({"seq": lax.rem(x + d, S)})
    greet({"attn": y * 2 + other})

    def load(src, at, size, dst, to, n):
        return pltpu.make_async_copy(src.at[pl.ds(at, size)], dst.at[pl.ds(to, size)], wsem.at[n])

    local = [
        pltpu.make_async_copy(tok, tok_blk.at[:, pl.ds(0, D)], wsem.at[0]),
        pltpu.make_async_copy(cot, cot_blk, wsem.at[1]),
        pltpu.make_async_copy(w_gt, gt, wsem.at[2]),
        pltpu.make_async_copy(w_ut, ut, wsem.at[3]),
        load(w_gs, 0, FT, wide, 0, 4),
        load(w_us, 0, FT, wide, FT, 5),
        load(w_gs, FT, FX, wide, 4 * FT, 6),
        load(w_us, FT, FX, wide, 4 * FT + FX, 7),
        load(w_ds, 0, FT, down, 0, 8),
        load(w_dt, 0, FT, down, FT, 9),
        load(w_ds, FT, FX, down, 2 * FT, 10),
    ]
    for copy in local:
        copy.start()

    local[0].wait()
    kind = jnp.concatenate(
        [jnp.full((1, LANE), mod[i].astype(F32), F32) for i in range(R)], axis=0
    )
    tok_blk[:, D:] = kind.astype(BF)
    local[1].wait()
    pl.semaphore_wait(barrier, 2 * W + (NY - 1) + (S - 1) + 1)

    def ahead(s):
        return lax.rem(z + E + (s + 1) // 2 * (2 * (s % 2) - 1), E)

    def mirror(s):
        return jnp.where(s == E - 1, s, s + 2 * (s % 2) - 1)

    pending = []

    def drain(keep=0):
        while len(pending) > keep:
            pending.pop(0)()

    def go(copy):
        copy.start()
        pending.append(copy.wait_send)

    def z_copy(k, s, src, dst, to):
        return remote(src(s), dst.at[to], zsem.at[k, 0, s], zsem.at[k, 1, to], {"exp": ahead(s)})

    def z_send(k, src, dst, low, high):
        def start(i, _):
            s = high - 1 - i
            z_copy(k, s, src, dst, mirror(s)).start()
            return 0

        def wait(s, _):
            z_copy(k, s, src, dst, s).wait_send()
            return 0

        lax.fori_loop(0, high - low, start, 0)
        pending.append(lambda: lax.fori_loop(low, high, wait, 0))

    def z_wait(k, src, dst, low, high):
        def wait(s, _):
            z_copy(k, s, src, dst, s).wait_recv()
            return 0

        lax.fori_loop(low, high, wait, 0)

    def y_copy(k, group, t, src, dst, mark):
        return remote(
            src, dst, ysem.at[k, group, 0, t], ysem.at[k, group, 1, mark], {"attn": t * 2 + c}
        )

    def g_copy(k, group, i, ref):
        return remote(
            ref, ref, gsem.at[k, group, 0, i], gsem.at[k, group, 1, i], {"attn": y * 2 + other}
        )

    def c_copy(k, n):
        w = pl.ds(n * NC, NC)
        return remote(
            sib_src.at[k, :, w], sib_dst.at[k, :, w], csem.at[k, 0, n], csem.at[k, 1, n],
            {"attn": y * 2 + other},
        )

    def x_copy(k, t, src, dst, mark):
        return remote(src, dst, xsem.at[k, 0, t], xsem.at[k, 1, mark], {"seq": t})

    def ys():
        return [lax.rem(y + d, NY) for d in far_first(NY)]

    def xs():
        return [lax.rem(x + d, S) for d in far_first(S)]

    def block(ref, core, yy, group):
        return ref.at[pl.ds(pl.multiple_of(core * HALF + yy * RB + group * RG, RG), RG)]

    def rows(ref, i):
        return ref.at[pl.ds(pl.multiple_of(i * CH, CH), CH)]

    def z_near(k, blk, buf):
        z_send(k, lambda s: blk, buf, 1, 2 * W + 1)

    def z_far(k, blk, buf):
        z_wait(k, lambda s: blk, buf, 2 * W - 1, 2 * W + 1)
        for j in range(W, 0, -1):
            for at, to, peer in (
                (2 * W, 2 * (W + j) if j < W else E - 1, z + j),
                (2 * W - 1, 2 * (W + j) - 1, z + E - j),
            )[: 2 if j < W else 1]:
                go(
                    remote(
                        buf.at[at], buf.at[to], zsem.at[k, 0, to], zsem.at[k, 1, to],
                        {"exp": lax.rem(peer, E)},
                    )
                )

    z_near(TOK, tok_blk, tok_z)
    z_near(COT, cot_blk, cot_z)
    tok_z[0] = tok_blk[...]
    cot_z[0] = cot_blk[...]
    local[2].wait()
    wide[2 * FT : 3 * FT, :] = gt[...].T
    local[3].wait()
    wide[3 * FT : 4 * FT, :] = ut[...].T

    def assemble(k, group, blk, buf, whole):
        low = group * (E // 2)
        if group == 0:
            z_wait(k, lambda s: blk, buf, 1, 2 * W - 1)
        else:
            z_wait(k, lambda s: blk, buf, 2 * W + 1, E)
        width = blk.shape[1]
        mine = block(whole, c, y, group)
        mine[...] = jnp.concatenate(
            [buf[low + i].astype(F32) for i in range(E // 2)], axis=0
        ).astype(BF)
        for t in ys():
            go(y_copy(k, group, t, mine, mine, y))
        go(g_copy(k, group, y, mine))

    def pass_on(k, group, whole):
        for t in reversed(ys()):
            got = block(whole, c, t, group)
            y_copy(k, group, t, got, got, t).wait_recv()
            go(g_copy(k, group, t, got))

    def from_sibling(k, whole):
        for group in range(2):
            for t in range(NY):
                g_copy(k, group, t, block(whole, other, t, group)).wait_recv()

    def half_rows(core):
        return pl.ds(pl.multiple_of(core * HALF, HALF), HALF)

    def project(core):
        r = half_rows(core)
        v = nt(xt[r, :D], wide[...])
        speech = xt[r, D:].astype(F32) < 0.5
        p1[r, 0:FT] = jnp.where(speech, v[:, :FT], v[:, 2 * FT : 3 * FT])
        p1[r, FT : 2 * FT] = jnp.where(speech, v[:, FT : 2 * FT], v[:, 3 * FT : 4 * FT])
        p1[r, 2 * FT :] = v[:, 4 * FT :]

    def x_half(k, core, src, dst):
        for t in xs():

            @pl.when(t // (S // 2) == core)
            def _():
                x_copy(k, t, rows(src, t), dst.at[x], x).start()

    def hidden_grad(core):
        r = half_rows(core)
        speech = xt[r, D:].astype(F32) < 0.5
        v = nt(ct[r, :], down[...])
        near = jnp.where(speech, v[:, :FT], v[:, FT : 2 * FT])
        tail = v[:, 2 * FT :]
        tail = jnp.concatenate([tail, jnp.zeros_like(tail)], axis=1)
        p2[r, 0:FT] = near
        p2[r, FT:] = tail

    z_far(TOK, tok_blk, tok_z)
    z_far(COT, cot_blk, cot_z)
    assemble(TOK, 0, tok_blk, tok_z, xt)
    assemble(TOK, 1, tok_blk, tok_z, xt)
    assemble(COT, 0, cot_blk, cot_z, ct)
    for copy in local[4:]:
        copy.wait()
    pass_on(TOK, 0, xt)
    assemble(COT, 1, cot_blk, cot_z, ct)
    pass_on(TOK, 1, xt)
    project(c)
    x_half(0, c, p1, r1)
    pass_on(COT, 0, ct)
    from_sibling(TOK, xt)
    project(other)
    x_half(0, other, p1, r1)
    pass_on(COT, 1, ct)
    hidden_grad(c)
    x_half(1, c, p2, r2)
    from_sibling(COT, ct)
    hidden_grad(other)
    x_half(1, other, p2, r2)
    for t in xs():
        pending.append(x_copy(0, t, rows(p1, t), r1.at[x], x).wait_send)
        pending.append(x_copy(1, t, rows(p2, t), r2.at[x], x).wait_send)

    def split(v):
        return v[:, :FX], v[:, FX : 2 * FX]

    total = rows(p1, x)[...]
    for t in xs():
        x_copy(0, t, r1.at[t], r1.at[t], t).wait_recv()
        total += r1[t]
    gu[...] = total
    g, u = total[:, :FT], total[:, FT : 2 * FT]
    ge, ue = split(total[:, 2 * FT :])
    he = jax.nn.silu(ge) * ue
    mine = rows(hb, x)
    mine[:, 0:FT] = (jax.nn.silu(g) * u).astype(BF)
    mine[:, FT:] = jnp.concatenate([he, jnp.zeros_like(he)], axis=1).astype(BF)
    for t in xs():
        go(x_copy(2, t, mine, mine, x))

    total = rows(p2, x)[...]
    for t in xs():
        x_copy(1, t, r2.at[t], r2.at[t], t).wait_recv()
        total += r2[t]

    def back(dh, g, u):
        sig = jax.nn.sigmoid(g)
        return dh * u * sig * (1.0 + g * (1.0 - sig)), dh * (g * sig)

    dg, du = back(total[:, :FT], gu[:, :FT], gu[:, FT : 2 * FT])
    ge, ue = split(gu[:, 2 * FT :])
    dge, due = back(total[:, FT : FT + FX], ge, ue)
    mine_g = rows(gb, x)
    mine_g[:, 0:FT] = dg.astype(BF)
    mine_g[:, FT : 2 * FT] = du.astype(BF)
    mine_g[:, 2 * FT :] = jnp.concatenate([dge, due], axis=1).astype(BF)
    for t in xs():
        go(x_copy(3, t, mine_g, mine_g, x))

    def kinds(r):
        text = xt[r, D:]
        return (1.0 - text.astype(F32)).astype(BF), text

    def out_left(core):
        r = half_rows(core)
        speech, text = kinds(r)
        h = hb[r, 0:FT]
        hcat[r, 0:FT] = h * speech
        hcat[r, FT : 2 * FT] = h * text
        hcat[r, 2 * FT :] = hb[r, FT : FT + FX] * speech[:, :FX]
        return hcat[r, :]

    def grad_left(core):
        r = half_rows(core)
        speech, text = kinds(r)
        dg, du = gb[r, 0:FT], gb[r, FT : 2 * FT]
        return jnp.concatenate(
            [dg * speech, du * speech, dg * text, du * text, gb[r, 2 * FT :] * speech], axis=1
        )

    def partials(k, left, weights):
        rows_other = left(other)
        for n in range(D // NC):
            w = slice(n * NC, (n + 1) * NC)
            sib_src[k, :, w] = nn(rows_other, weights[:, w]).astype(BF)
            go(c_copy(k, n))
        rows_own = left(c)
        for n in range(D // NC):
            w = slice(n * NC, (n + 1) * NC)
            acc[k, :, w] = nn(rows_own, weights[:, w])

    def part(ref, k, t, group):
        return ref.at[k, pl.ds(pl.multiple_of(t * RB + group * RG, RG), RG)]

    def over_y(k):
        for n in range(D // NC):
            c_copy(k, n).wait_recv()
        for group in (1, 0):
            for t in ys():
                v = part(acc, k, t, group)[...] + part(sib_dst, k, t, group)[...].astype(F32)
                part(y_src, k, t, group)[...] = v.astype(BF)
                go(y_copy(2 + k, group, t, part(y_src, k, t, group), y_dst.at[k, group, y], y))

    def over_z(k):
        for group in (1, 0):
            total = part(acc, k, y, group)[...] + part(sib_dst, k, y, group)[...].astype(F32)
            for t in reversed(ys()):
                got = y_dst.at[k, group, t]
                y_copy(2 + k, group, t, got, got, t).wait_recv()
                total += got[...].astype(F32)
            low = group * (E // 2)
            for i in range(E // 2):
                z_src[k, low + i] = total[i * R : (i + 1) * R].astype(BF)
            z_send(2 + k, lambda s: z_src.at[k, s], z_dst.at[k], max(low, 1), low + E // 2)

    def finish(k, out):
        z_wait(2 + k, lambda s: z_src.at[k, s], z_dst.at[k], 1, E)
        total = z_src[k, 0].astype(F32)
        for i in range(1, E):
            total += z_dst[k, i].astype(F32)
        out[...] = total.astype(BF)

    def down_grads():
        left = hcat[...].T

        def body(n, _):
            w = pl.ds(pl.multiple_of(n * NC, NC), NC)
            v = nn(left, ct[:, w]).astype(BF)
            dsg[0:FT, w] = v[0:FT]
            dtg[:, w] = v[FT : 2 * FT]
            dsg[FT:, w] = v[2 * FT :]
            return 0

        lax.fori_loop(0, D // NC, body, 0)

    for t in xs():
        got = rows(hb, t)
        x_copy(2, t, got, got, t).wait_recv()
    partials(0, out_left, down)
    before = len(pending)
    over_y(0)
    sent_y = len(pending) - before + D // NC
    down_grads()
    for t in xs():
        got = rows(gb, t)
        x_copy(3, t, got, got, t).wait_recv()
    partials(1, grad_left, wide)
    before = len(pending)
    over_y(1)
    drain(len(pending) - before + sent_y)
    over_z(0)
    over_z(1)
    drain(2)
    finish(0, mixed)
    drain()
    finish(1, grad)

    drain()


def place(*refs):
    sem, copies = refs[8], []
    for src, dst in zip(refs[:4], refs[4:8]):
        strip = 64 if src.shape[0] % 64 == 0 else src.shape[0]
        for i in range(0, src.shape[0], strip):
            part = pl.ds(i, strip)
            copies.append(pltpu.make_async_copy(src.at[part], dst.at[part], sem.at[len(copies)]))
    for copy in copies:
        copy.start()
    for copy in copies:
        copy.wait()


def shards(NY, E, S, tokens, modality, cotangent, *weights):
    R, D = tokens.shape
    gs, us, ds, gt, ut, dt = weights
    gs, us = gs.T, us.T
    FS, FT = gs.shape[0], gt.shape[1]
    RB = E * R
    HALF = NY * RB
    T = 2 * HALF
    CH = T // S
    DMA = pltpu.SemaphoreType.DMA
    hbm_spec = pl.BlockSpec(memory_space=pltpu.HBM)
    vmem_spec = pl.BlockSpec(memory_space=pltpu.VMEM)
    out_shape = (
        jax.ShapeDtypeStruct((R, D), BF),
        jax.ShapeDtypeStruct((R, D), BF),
        jax.ShapeDtypeStruct(ds.shape, BF),
        jax.ShapeDtypeStruct(dt.shape, BF),
    )
    outs = pl.pallas_call(
        functools.partial(kernel, NY, E, S),
        out_shape=tuple(pltpu.VMEM(o.shape, BF) for o in out_shape),
        in_specs=[hbm_spec, pl.BlockSpec(memory_space=pltpu.SMEM)] + [hbm_spec] * 7,
        out_specs=[vmem_spec] * 4,
        scratch_shapes=[
            pltpu.VMEM(gt.shape, BF),
            pltpu.VMEM(ut.shape, BF),
            pltpu.VMEM((2 * (FS + FT), D), BF),
            pltpu.VMEM((FS + FT, D), BF),
            pltpu.VMEM((R, D + LANE), BF),
            pltpu.VMEM((R, D), BF),
            pltpu.VMEM((E, R, D + LANE), BF),
            pltpu.VMEM((E, R, D), BF),
            pltpu.VMEM((T, D + LANE), BF),
            pltpu.VMEM((T, D), BF),
            pltpu.VMEM((T, 3 * FT), F32),
            pltpu.VMEM((T, 2 * FT), F32),
            pltpu.VMEM((S, CH, 3 * FT), F32),
            pltpu.VMEM((S, CH, 2 * FT), F32),
            pltpu.VMEM((CH, 3 * FT), F32),
            pltpu.VMEM((T, 2 * FT), BF),
            pltpu.VMEM((T, 3 * FT), BF),
            pltpu.VMEM((2, HALF, D), BF),
            pltpu.VMEM((2, HALF, D), BF),
            pltpu.VMEM((2, HALF, D), F32),
            pltpu.VMEM((2, HALF, D), BF),
            pltpu.VMEM((2, 2, NY, RB // 2, D), BF),
            pltpu.VMEM((2, E, R, D), BF),
            pltpu.VMEM((2, E, R, D), BF),
            pltpu.VMEM((T, FS + FT), BF),
            DMA((11,)),
            DMA((4, 2, E)),
            DMA((4, 2, 2, NY)),
            DMA((2, 2, 2, NY)),
            DMA((2, 2, 8)),
            DMA((4, 2, S)),
        ],
        compiler_params=pltpu.CompilerParams(
            collective_id=0, has_side_effects=True, vmem_limit_bytes=58 << 20
        ),
    )(tokens, modality, cotangent, gs, us, ds, gt, ut, dt)
    return pl.pallas_call(
        place,
        out_shape=out_shape,
        in_specs=[vmem_spec] * 4,
        out_specs=[hbm_spec] * 4,
        scratch_shapes=[DMA((16,))],
        compiler_params=pltpu.CompilerParams(vmem_limit_bytes=16 << 20),
    )(*outs)


def solution(mesh):
    NY, E, S = mesh.shape["attn"] // 2, mesh.shape["exp"], mesh.shape["seq"]
    row = P(("attn", "exp"), "seq")
    col = P("seq", ("attn", "exp"))
    return jax.shard_map(
        functools.partial(shards, NY, E, S),
        mesh=mesh,
        in_specs=(row, P(("attn", "exp")), row, col, col, row, col, col, row),
        out_specs=(row, row, row, row),
        check_vma=False,
    )
```
